128 devices in a mesh: row: 16 (over x, z), col: 8 (over y, core).
Axes of the slice: x: 4, y: 4, z: 4, core: 2. Of those that a mesh axis runs over, the one named last changes fastest.
Arguments:
- tokens: bfloat16 [512, 256, 384], P('row', 'col'), may hold values from -6 to 6
- first_gain: float32 [384], replicated, may hold values from 0.1 to 1.9
- second_gain: float32 [384], replicated, may hold values from 0.1 to 1.9
- joint_weight: bfloat16 [384, 1152], replicated, may hold values from -0.3125 to 0.3125
- merge_weight: bfloat16 [384, 384], replicated, may hold values from -0.3125 to 0.3125
- expand_weight: bfloat16 [384, 1536], replicated, may hold values from -0.3125 to 0.3125
- shrink_weight: bfloat16 [1536, 384], replicated, may hold values from -0.15625 to 0.15625
- relative_bias: float32 [12, 64, 64], replicated, may hold values from -4 to 270
- lateral_weight: bfloat16 [384, 256], replicated, may hold values from -0.3125 to 0.3125
- conv_weight: bfloat16 [4, 2304, 256], replicated, may hold values from -0.125 to 0.125
- mask_weight: bfloat16 [256], replicated, may hold values from -0.375 to 0.375
- box_geometry: int32 [16, 8, 16, 4], P('row', 'col'), may hold values from 0 to 18, as said below
- box_counts: int32 [16, 8], P('row', 'col'), may hold values from 0 to 16, as said below
- box_owner: int32 [16, 8, 16], P('row', 'col'), may hold values from -1 to 15, as said below
- soft_target: bfloat16 [16, 8, 16, 196], P('row', 'col'), may hold values from 0 to 1
Outputs:
- features: bfloat16 [512, 256, 256], P('row', 'col')
- feature_grad: float32 [512, 256, 256], P('row', 'col')
- mask_logits: float32 [16, 8, 8, 196], P('row', 'col')
The draws below stay inside these ranges and needn't reach their ends.
Inputs may be any that keep to these rules, and one draw needn't show every extreme that they name: `box_geometry`: components are top from 0 to 18, left from 0 to 18, height and width from 4 to 14; every slot, used or not, holds such a box. `box_counts`: the counts of one tile column sum to 8 times the tiles along the column; some tile of every column holds exactly 16 boxes. `box_owner`: A slot at or beyond its tile's count holds -1, a used slot an owner in its tile column; every owner is named by exactly 8 boxes of its column, and a tile names one owner at most 1 times, a bound reached by every tile holding 16 boxes.
All inputs are finite; a program needn't handle non-finite values.
Results may differ from the reference program's by a relative error of at most 0.02.
Values may be sent and summed in bfloat16 or wider, within the bound.
A program may use at most 128 MiB of HBM per device.

```python
import jax
import jax.numpy as jnp
from jax import lax

C = 384
HEADS = 12
FF = 1536
F = 256
HEAD_DIM = 32
WIN = 8
SHIFT = 4
TILE_R = 32
TILE_C = 32
CROP = 14
MIN_SIDE = 4
CONV_LAYERS = 4
BOX_OWN = 8
CAP = 16
TILES_DOWN = 16
TILES_ACROSS = 8
GRID_ROWS = 512
GRID_COLS = 256


def box_plan(key):
    base = jax.random.fold_in(key, 11)
    order_keys = jax.random.split(jax.random.fold_in(base, 1), TILES_ACROSS)
    owner_keys = jax.random.split(jax.random.fold_in(base, 2), TILES_ACROSS)
    tile_order = jax.vmap(lambda single_key: jax.random.permutation(single_key, TILES_DOWN))(order_keys).astype(jnp.int32)
    owner_order = jax.vmap(lambda single_key: jax.random.permutation(single_key, TILES_DOWN))(owner_keys).astype(jnp.int32)
    moved = jax.random.randint(jax.random.fold_in(base, 3), (TILES_ACROSS, TILES_DOWN // 2), 0, BOX_OWN + 1)
    moved = moved.at[:, 0].set(BOX_OWN)
    signs = 2 * jax.random.randint(jax.random.fold_in(base, 4), (TILES_ACROSS, TILES_DOWN // 2), 0, 2) - 1
    paired = jnp.stack([BOX_OWN + signs * moved, BOX_OWN - signs * moved], axis=2).reshape(TILES_ACROSS, TILES_DOWN)
    column_index = jnp.broadcast_to(jnp.arange(TILES_ACROSS, dtype=jnp.int32)[:, None], (TILES_ACROSS, TILES_DOWN))
    counts = jnp.zeros((TILES_ACROSS, TILES_DOWN), jnp.int32).at[column_index, tile_order].set(paired.astype(jnp.int32))
    counts = counts.T
    starts = jnp.cumsum(counts, axis=0) - counts
    slot_range = jnp.arange(CAP, dtype=jnp.int32)
    sequence = (starts[:, :, None] + slot_range[None, None, :]) % TILES_DOWN
    column_grid = jnp.broadcast_to(jnp.arange(TILES_ACROSS, dtype=jnp.int32)[None, :, None], sequence.shape)
    owner = owner_order[column_grid, sequence]
    owner = jnp.where(slot_range[None, None, :] < counts[:, :, None], owner, -1)
    return (counts.astype(jnp.int32), owner.astype(jnp.int32))


def draw_box_counts(key, part):
    return box_plan(key)[0]


def draw_box_owner(key, part):
    return box_plan(key)[1]


def draw_box_geometry(key, part):
    base = jax.random.fold_in(key, 23)
    shape = (TILES_DOWN, TILES_ACROSS, CAP)
    upper = jax.random.randint(jax.random.fold_in(base, 1), shape, 0, TILE_R - CROP + 1)
    leftmost = jax.random.randint(jax.random.fold_in(base, 2), shape, 0, TILE_C - CROP + 1)
    tall = jax.random.randint(jax.random.fold_in(base, 3), shape, MIN_SIDE, CROP + 1)
    broad = jax.random.randint(jax.random.fold_in(base, 4), shape, MIN_SIDE, CROP + 1)
    return jnp.stack([upper, leftmost, tall, broad], axis=-1).astype(jnp.int32)


def draw_relative_bias(key, part):
    base = jax.random.fold_in(key, 37)
    positions = WIN * WIN
    return jnp.clip(jax.random.normal(jax.random.fold_in(base, 6), (HEADS, positions, positions), jnp.float32), -4.0, 4.0)


def block_levels(own_key, dims, cuts, low, largest):
    level = 1.0
    for dim, blocks in cuts:
        heights = jax.random.uniform(jax.random.fold_in(jax.random.fold_in(own_key, 6), dim), (blocks,), jnp.float32, low / len(cuts), largest / len(cuts))
        level = level * jnp.repeat(jnp.exp(heights), dims[dim] // blocks).reshape((-1,) + (1,) * (len(dims) - 1 - dim))
    return level


def scatter_about(stream_key, dims, scale, limit, cuts=(), kind=jnp.bfloat16):
    result = scale * jax.random.normal(stream_key, dims, jnp.float32)
    if cuts:
        result = result * block_levels(stream_key, dims, cuts, -0.22, 0.18)
    return jnp.clip(result, -limit, limit).astype(kind)


def setup_inputs(seed: int = 0) -> dict:
    key_of = jax.random.split(jax.random.key(seed), 16)
    tokens = scatter_about(key_of[0], (GRID_ROWS, GRID_COLS, C), 1.0, 6.0, ((0, 16), (1, 8)))
    first_gain = jnp.clip(1.0 + 0.18 * jax.random.normal(key_of[1], (C,), jnp.float32), 0.1, 1.9)
    second_gain = jnp.clip(1.0 + 0.18 * jax.random.normal(key_of[2], (C,), jnp.float32), 0.1, 1.9)
    joint_weight = scatter_about(key_of[3], (C, 3 * C), C ** -0.5, 0.3125)
    merge_weight = scatter_about(key_of[4], (C, C), C ** -0.5, 0.3125)
    expand_weight = scatter_about(key_of[5], (C, FF), C ** -0.5, 0.3125)
    shrink_weight = scatter_about(key_of[6], (FF, C), FF ** -0.5, 0.15625)
    relative_bias = draw_relative_bias(jax.random.fold_in(key_of[15], 71), 0)
    lateral_weight = scatter_about(key_of[8], (C, F), C ** -0.5, 0.3125)
    conv_weight = scatter_about(key_of[9], (CONV_LAYERS, 9 * F, F), (9 * F) ** -0.5, 0.125)
    mask_weight = scatter_about(key_of[10], (F,), F ** -0.5, 0.375)
    box_geometry = draw_box_geometry(jax.random.fold_in(key_of[15], 71), 0)
    box_counts = draw_box_counts(jax.random.fold_in(key_of[15], 71), 0)
    box_owner = draw_box_owner(jax.random.fold_in(key_of[15], 71), 0)
    soft_target = jnp.clip(1.0 * jax.random.uniform(key_of[14], (TILES_DOWN, TILES_ACROSS, CAP, CROP * CROP), jnp.float32) ** block_levels(key_of[14], (TILES_DOWN, TILES_ACROSS, CAP, CROP * CROP), ((0, 16), (1, 8)), -0.2, 0.2), 0.0, 1.0).astype(jnp.bfloat16)
    return {"tokens": tokens, "first_gain": first_gain, "second_gain": second_gain, "joint_weight": joint_weight, "merge_weight": merge_weight, "expand_weight": expand_weight, "shrink_weight": shrink_weight, "relative_bias": relative_bias, "lateral_weight": lateral_weight, "conv_weight": conv_weight, "mask_weight": mask_weight, "box_geometry": box_geometry, "box_counts": box_counts, "box_owner": box_owner, "soft_target": soft_target}


EPSILON = 1e-05
loss_scale = 128.0

def layer_norm(values, gain):
    values = values.astype(jnp.float32)
    centered = values - lax.optimization_barrier(jnp.mean(values, axis=-1, keepdims=True))
    variance = lax.optimization_barrier(jnp.mean(centered * centered, axis=-1, keepdims=True))
    return centered * lax.rsqrt(variance + EPSILON) * gain

def swin_strip(strip_rows, labels, first_gain, second_gain, joint_weight, merge_weight, expand_weight, shrink_weight, relative_bias):
    width_model = strip_rows.shape[-1]
    windows = strip_rows.shape[1] // WIN
    normed = layer_norm(strip_rows, first_gain).astype(jnp.bfloat16)
    joint = jnp.dot(normed.reshape(-1, width_model), joint_weight, preferred_element_type=jnp.float32).astype(jnp.bfloat16)
    joint = joint.reshape(WIN, windows, WIN, 3, HEADS, HEAD_DIM).transpose(1, 0, 2, 3, 4, 5)
    joint = joint.reshape(windows, WIN * WIN, 3, HEADS, HEAD_DIM)
    window_labels = labels.reshape(WIN, windows, WIN).transpose(1, 0, 2).reshape(windows, WIN * WIN)
    queries = joint[:, :, 0].astype(jnp.float32)
    key_rows = joint[:, :, 1].astype(jnp.float32)
    value_rows = joint[:, :, 2].astype(jnp.float32)
    scores = jnp.einsum('wqhd,wkhd->whqk', queries, key_rows) * HEAD_DIM ** (-0.5) + relative_bias[None]
    allowed = window_labels[:, None, :, None] == window_labels[:, None, None, :]
    scores = jnp.where(allowed, scores, -1000000000.0)
    highest = lax.optimization_barrier(jnp.max(scores, axis=-1, keepdims=True))
    weights = jnp.exp(scores - highest)
    probabilities = (weights / lax.optimization_barrier(jnp.sum(weights, axis=-1, keepdims=True))).astype(jnp.bfloat16)
    mixed = jnp.einsum('whqk,wkhd->wqhd', probabilities.astype(jnp.float32), value_rows).astype(jnp.bfloat16)
    mixed = mixed.reshape(windows, WIN, WIN, width_model).transpose(1, 0, 2, 3).reshape(-1, width_model)
    residual = strip_rows.reshape(-1, width_model).astype(jnp.float32) + jnp.dot(mixed, merge_weight, preferred_element_type=jnp.float32)
    normed_second = layer_norm(residual, second_gain).astype(jnp.bfloat16)
    hidden = jax.nn.gelu(jnp.dot(normed_second, expand_weight, preferred_element_type=jnp.float32)).astype(jnp.bfloat16)
    block_out = (residual + jnp.dot(hidden, shrink_weight, preferred_element_type=jnp.float32)).astype(jnp.bfloat16)
    return block_out.reshape(WIN, -1, width_model)

def conv_forward(activation, kernel):
    padded = jnp.pad(activation, ((0, 0), (1, 1), (1, 1), (0, 0)))
    columns = jnp.concatenate([padded[:, row_off:row_off + CROP, col_off:col_off + CROP, :] for row_off in range(3) for col_off in range(3)], axis=-1)
    product = jnp.dot(columns.reshape(-1, columns.shape[-1]), kernel, preferred_element_type=jnp.float32)
    return product.reshape(activation.shape[0], CROP, CROP, -1)

def conv_backward(grad_before, kernel):
    channels = kernel.shape[-1]
    spread = jnp.dot(grad_before.reshape(-1, channels), kernel.T, preferred_element_type=jnp.float32)
    spread = spread.reshape(grad_before.shape[0], CROP, CROP, 9, channels)
    padded = jnp.pad(spread, ((0, 0), (1, 1), (1, 1), (0, 0), (0, 0)))
    summed = jnp.zeros((grad_before.shape[0], CROP, CROP, channels), jnp.float32)
    for row_off in range(3):
        for col_off in range(3):
            summed = summed + padded[:, 2 - row_off:2 - row_off + CROP, 2 - col_off:2 - col_off + CROP, row_off * 3 + col_off]
    return summed

def mask_head(crops, box_maps, conv_weight, mask_weight):
    activation = crops
    pre_stack = []
    for layer_index in range(conv_weight.shape[0]):
        before = conv_forward(activation, conv_weight[layer_index])
        pre_stack.append(before)
        activation = jax.nn.gelu(before).astype(jnp.bfloat16)
    channels = activation.shape[-1]
    logits = jnp.dot(activation.reshape(-1, channels), mask_weight, preferred_element_type=jnp.float32).reshape(activation.shape[0], -1)
    target = box_maps[:, 0]
    inside = box_maps[:, 1]
    grad_logits = loss_scale * (jax.nn.sigmoid(logits) - target) * inside
    grad_activation = grad_logits.reshape(activation.shape[:3])[..., None] * mask_weight.astype(jnp.float32)
    for layer_index in reversed(range(conv_weight.shape[0])):
        grad_before = jax.vjp(jax.nn.gelu, pre_stack[layer_index])[1](grad_activation)[0].astype(jnp.bfloat16)
        grad_activation = conv_backward(grad_before, conv_weight[layer_index])
    crop_grad = grad_activation * inside.reshape(-1, CROP, CROP)[..., None]
    return (logits, crop_grad)

def reference(tokens, first_gain, second_gain, joint_weight, merge_weight, expand_weight, shrink_weight, relative_bias, lateral_weight, conv_weight, mask_weight, box_geometry, box_counts, box_owner, soft_target):
    grid_rows = tokens.shape[0]
    grid_cols = tokens.shape[1]
    rolled = jnp.roll(tokens, (-SHIFT, -SHIFT), axis=(0, 1))
    col_wrap = (jnp.arange(grid_cols, dtype=jnp.int32) >= grid_cols - SHIFT).astype(jnp.int32)

    def one_strip(strip_index):
        strip_rows = lax.dynamic_slice_in_dim(rolled, strip_index * WIN, WIN, 0)
        row_wrap = (strip_index * WIN + jnp.arange(WIN, dtype=jnp.int32) >= grid_rows - SHIFT).astype(jnp.int32)
        labels = 2 * row_wrap[:, None] + col_wrap[None, :]
        return swin_strip(strip_rows, labels, first_gain, second_gain, joint_weight, merge_weight, expand_weight, shrink_weight, relative_bias)
    strips = lax.map(one_strip, jnp.arange(grid_rows // WIN, dtype=jnp.int32))
    block_out = jnp.roll(strips.reshape(grid_rows, grid_cols, -1), (SHIFT, SHIFT), axis=(0, 1))
    features = jnp.dot(block_out.reshape(-1, block_out.shape[-1]), lateral_weight, preferred_element_type=jnp.float32)
    features = features.astype(jnp.bfloat16).reshape(grid_rows, grid_cols, -1)
    channels = features.shape[-1]
    slot_range = jnp.arange(CAP, dtype=jnp.int32)
    is_valid = slot_range[None, None, :] < box_counts[:, :, None]
    owner_list = jnp.where(is_valid, box_owner, -1)
    column_major = owner_list.transpose(1, 0, 2).reshape(TILES_ACROSS, TILES_DOWN * CAP)
    hits = (column_major[:, :, None] == jnp.arange(TILES_DOWN, dtype=jnp.int32)[None, None, :]).astype(jnp.int32)
    earlier = jnp.cumsum(hits, axis=1) - hits
    position = lax.optimization_barrier(jnp.sum(earlier * hits, axis=2)).astype(jnp.int32)
    flat_ids = (jnp.arange(TILES_DOWN, dtype=jnp.int32)[None, :, None] * TILES_ACROSS + jnp.arange(TILES_ACROSS, dtype=jnp.int32)[:, None, None]) * CAP + slot_range[None, None, :]
    flat_ids = flat_ids.reshape(TILES_ACROSS, TILES_DOWN * CAP).astype(jnp.int32)
    owner_row = jnp.where(column_major >= 0, column_major, TILES_DOWN).astype(jnp.int32)
    column_index = jnp.broadcast_to(jnp.arange(TILES_ACROSS, dtype=jnp.int32)[:, None], owner_row.shape)
    table = jnp.zeros((TILES_DOWN, TILES_ACROSS, BOX_OWN), jnp.int32).at[owner_row, column_index, position].set(flat_ids, mode='drop')
    geometry_flat = box_geometry.reshape(-1, 4)
    targets_flat = soft_target.reshape(-1, CROP * CROP)
    offsets = jnp.arange(CROP, dtype=jnp.int32)

    def box_anchor(box_ids):
        tile_row = box_ids // (TILES_ACROSS * CAP)
        tile_col = box_ids // CAP % TILES_ACROSS
        geometry = geometry_flat[box_ids]
        return ((tile_row * TILE_R + geometry[:, 0]).astype(jnp.int32), (tile_col * TILE_C + geometry[:, 1]).astype(jnp.int32), geometry)

    def one_group(box_ids):
        row_start, col_start, geometry = box_anchor(box_ids)

        def cut(start_row, start_col):
            return lax.dynamic_slice(features, (start_row, start_col, jnp.int32(0)), (CROP, CROP, channels))
        crops = jax.vmap(cut)(row_start, col_start)
        inside = (offsets[None, :, None] < geometry[:, 2, None, None]) & (offsets[None, None, :] < geometry[:, 3, None, None])
        crops = jnp.where(inside[..., None], crops, jnp.zeros((), crops.dtype))
        box_maps = jnp.stack([targets_flat[box_ids].astype(jnp.float32), inside.reshape(-1, CROP * CROP).astype(jnp.float32)], axis=1)
        return mask_head(crops, box_maps, conv_weight, mask_weight)
    logits, crop_grad = lax.map(one_group, table.reshape(TILES_DOWN * TILES_ACROSS, BOX_OWN))
    mask_logits = logits.reshape(TILES_DOWN, TILES_ACROSS, BOX_OWN, CROP * CROP)
    all_ids = table.reshape(-1)
    row_start, col_start, geometry = box_anchor(all_ids)
    row_index = jnp.broadcast_to(row_start[:, None, None] + offsets[None, :, None], (all_ids.shape[0], CROP, CROP))
    col_index = jnp.broadcast_to(col_start[:, None, None] + offsets[None, None, :], (all_ids.shape[0], CROP, CROP))
    feature_grad = jnp.zeros((grid_rows, grid_cols, channels), jnp.float32).at[row_index, col_index].add(crop_grad.reshape(-1, CROP, CROP, channels))
    return (features, feature_grad, mask_logits)
```

```python
import functools
import jax
import jax.numpy as jnp
from jax import lax
from jax.experimental import pallas as pl
from jax.experimental.pallas import tpu as pltpu
from jax.sharding import PartitionSpec as P

HEADS = 12
WIN = 8
CROP = 14
BOX_OWN = 8


EPSILON = 1e-05
loss_scale = 128.0


def with_halo(x, sides, width):
    for axis, dim in sides:
        size, length = (lax.axis_size(axis), x.shape[dim])
        up = [(i, (i + 1) % size) for i in range(size - 1)]
        down = [(j, i) for i, j in up]
        last = lax.slice_in_dim(x, length - width, length, axis=dim)
        first = lax.slice_in_dim(x, 0, width, axis=dim)
        before = lax.ppermute(last, axis, up)
        after = lax.ppermute(first, axis, down)
        x = jnp.concatenate([before, x, after], axis=dim)
    return x


def layer_norm(values, gain):
    values = values.astype(jnp.float32)
    centered = values - jnp.mean(values, axis=-1, keepdims=True)
    variance = jnp.mean(centered * centered, axis=-1, keepdims=True)
    return centered * lax.rsqrt(variance + EPSILON) * gain


def to_windows(grid):
    grid_height, grid_width, depth_size = grid.shape
    grid = grid.reshape(grid_height // WIN, WIN, grid_width // WIN, WIN, depth_size).transpose(
        0, 2, 1, 3, 4
    )
    return grid.reshape(-1, WIN * WIN, depth_size)


def from_windows(windows, grid_height, grid_width):
    depth_size = windows.shape[-1]
    grid = windows.reshape(grid_height // WIN, grid_width // WIN, WIN, WIN, depth_size).transpose(
        0, 2, 1, 3, 4
    )
    return grid.reshape(grid_height, grid_width, depth_size)


def attend(joint, labels, relative_bias):
    queries = joint[:, :, 0]
    key_rows = joint[:, :, 1]
    value_rows = joint[:, :, 2]
    head_size = queries.shape[-1]
    scores = jnp.einsum("wqhd,wkhd->whqk", queries, key_rows, preferred_element_type=jnp.float32)
    scores = scores * head_size ** (-0.5) + relative_bias[None]
    allowed = labels[:, None, :, None] == labels[:, None, None, :]
    scores = jnp.where(allowed, scores, -1000000000.0)
    highest = jnp.max(scores, axis=-1, keepdims=True)
    weights = jnp.exp(scores - highest)
    probabilities = (weights / jnp.sum(weights, axis=-1, keepdims=True)).astype(jnp.bfloat16)
    mixed = jnp.einsum(
        "whqk,wkhd->wqhd", probabilities, value_rows, preferred_element_type=jnp.float32
    ).astype(jnp.bfloat16)
    return mixed.reshape(mixed.shape[0], mixed.shape[1], -1)


K1C = 0.7978845608028654
K2C = 0.044715
ROWS = 224

def gelu_pair(x):
    x2 = x * x
    inner = x * (K1C + (K1C * K2C) * x2)
    th = jnp.tanh(inner)
    half = 0.5 + 0.5 * th
    act = x * half
    slope = half + (0.5 * x) * (1.0 - th * th) * (K1C + (3.0 * K1C * K2C) * x2)
    return act, slope

def mask_kernel(U, gs, cs, geom, feat, w, mw, tgt, fg, lg, X, Y, D):
    f32, bf16 = jnp.float32, jnp.bfloat16
    cnt = cs[0, 0]
    zrow = jnp.zeros((256, 256), bf16)
    for B in (X, Y):
        B[0] = zrow
        B[15] = zrow
        for u in range(1, 15):
            B[u, 0:16, :] = zrow[0:16]
            B[u, 240:256, :] = zrow[0:16]
    g = geom[...]
    valid = lax.broadcasted_iota(jnp.int32, (16, 1), 0) < cnt
    rep = lambda col: jnp.concatenate([col] * 14, axis=0)
    lefts, widths = rep(g[:, 1:2]), rep(g[:, 3:4])
    heights = rep(jnp.where(valid, g[:, 2:3], 0))
    row = lax.broadcasted_iota(jnp.int32, (ROWS, 1), 0)
    vv, kk = row // 16, row % 16
    target = jnp.where(vv < widths, kk * 32 + lefts + vv, -1)
    lane = lax.broadcasted_iota(jnp.int32, (ROWS, 512), 1)
    pick = jnp.where(lane == target, 1.0, 0.0).astype(bf16)
    in_w = vv < widths

    def gather(u, c):
        strips = jnp.concatenate([feat[gs[k, 0] + u] for k in range(16)], axis=0)
        crop = jnp.dot(pick, strips, preferred_element_type=f32)
        crop = jnp.where(u < heights, crop, 0.0)
        X[u + 1, 16:240, :] = crop.astype(bf16)
        return c
    lax.fori_loop(0, 14, gather, 0)

    def fwd(src, dst, l):
        def body(i, c):
            u0 = i * U
            cols = []
            for s in range(3):
                for t in range(3):
                    cols.append(jnp.concatenate([src[u0 + q + s, t * 16:t * 16 + ROWS, :] for q in range(U)], axis=0))
            pre = jnp.dot(jnp.concatenate(cols, axis=1), w[l], preferred_element_type=f32)
            act, slope = gelu_pair(pre)
            for q in range(U):
                a = act[q * ROWS:(q + 1) * ROWS].astype(bf16)
                sl = slope[q * ROWS:(q + 1) * ROWS]
                if l < 3:
                    dst[u0 + q + 1, 16:240, :] = a
                    D[l, u0 + q] = sl.astype(bf16)
                else:
                    u = u0 + q
                    m = mw[...].astype(f32)
                    logit = jnp.sum(a.astype(f32) * m, axis=1, keepdims=True)
                    sel = lax.broadcasted_iota(jnp.int32, (ROWS, 128), 1) == u
                    lg[...] = jnp.where(sel, logit, lg[...])
                    tg = jnp.sum(jnp.where(sel, tgt[...], 0.0), axis=1, keepdims=True)
                    gl = jnp.where(in_w & (u < heights), 128.0 * (jax.nn.sigmoid(logit) - tg), 0.0)
                    dst[u + 1, 16:240, :] = (gl * m * sl).astype(bf16)
            return c
        lax.fori_loop(0, 14 // U, body, 0)

    lg[...] = jnp.zeros_like(lg)
    fwd(X, Y, 0)
    fwd(Y, X, 1)
    fwd(X, Y, 2)
    fwd(Y, X, 3)

    fg[...] = jnp.zeros_like(fg)

    def bwd(src, dst, l):
        def body(i, c):
            u0 = i * U
            acc = None
            for s in range(3):
                for t in range(3):
                    a = jnp.concatenate([src[u0 + q + 2 - s, (2 - t) * 16:(2 - t) * 16 + ROWS, :] for q in range(U)], axis=0)
                    tap = 3 * s + t
                    d = lax.dot_general(a, w[l, tap * 256:(tap + 1) * 256, :], (((1,), (1,)), ((), ())), preferred_element_type=f32)
                    acc = d if acc is None else acc + d
            for q in range(U):
                gq = acc[q * ROWS:(q + 1) * ROWS]
                if l > 0:
                    dst[u0 + q + 1, 16:240, :] = (gq * D[l - 1, u0 + q].astype(f32)).astype(bf16)
                else:
                    u = u0 + q
                    gq = jnp.where(u < heights, gq, 0.0).astype(bf16)
                    z = lax.dot_general(pick, gq, (((0,), (0,)), ((), ())), preferred_element_type=f32)
                    for k in range(16):
                        fg[gs[k, 0] + u] += z[k * 32:(k + 1) * 32]
            return c
        lax.fori_loop(0, 14 // U, body, 0)
    bwd(X, Y, 3)
    bwd(Y, X, 2)
    bwd(X, Y, 1)
    bwd(Y, X, 0)

def mask_head(U, geometry, count, feat, conv_w, mask_w, tgt):
    V = pl.BlockSpec(memory_space=pltpu.VMEM)
    S = pl.BlockSpec(memory_space=pltpu.SMEM)
    return pl.pallas_call(
        functools.partial(mask_kernel, U),
        out_shape=(jax.ShapeDtypeStruct((32, 32, 256), jnp.float32), jax.ShapeDtypeStruct((ROWS, 128), jnp.float32)),
        in_specs=[S, S, V, V, V, V, V],
        out_specs=(V, V),
        scratch_shapes=[pltpu.VMEM((16, 256, 256), jnp.bfloat16), pltpu.VMEM((16, 256, 256), jnp.bfloat16), pltpu.VMEM((3, 14, ROWS, 256), jnp.bfloat16)],
        compiler_params=pltpu.CompilerParams(vmem_limit_bytes=60 << 20),
    )(geometry, count, geometry, feat, conv_w, mask_w, tgt)


def compact_order(present):
    present_int = present.astype(jnp.int32)
    position = jnp.cumsum(present_int) - present_int
    picker = (position[None, :] == jnp.arange(BOX_OWN, dtype=jnp.int32)[:, None]) & present[None, :]
    return picker


def shards(
    tokens,
    first_gain,
    second_gain,
    joint_weight,
    merge_weight,
    expand_weight,
    shrink_weight,
    relative_bias,
    lateral_weight,
    conv_weight,
    mask_weight,
    box_geometry,
    box_counts,
    box_owner,
    soft_target,
):
    tile_rows, tile_cols, width_model = tokens.shape
    shift_size = WIN // 2
    row_anchor = lax.axis_index("row") * tile_rows
    col_anchor = lax.axis_index("col") * tile_cols
    grid_rows = tile_rows * lax.axis_size("row")
    grid_cols = tile_cols * lax.axis_size("col")
    extended = with_halo(tokens, (("row", 0), ("col", 1)), shift_size)
    ext_rows = tile_rows + 2 * shift_size
    ext_cols = tile_cols + 2 * shift_size
    normed = layer_norm(extended, first_gain).astype(jnp.bfloat16)
    joint = jnp.dot(
        normed.reshape(-1, width_model), joint_weight, preferred_element_type=jnp.float32
    ).astype(jnp.bfloat16)
    joint = to_windows(joint.reshape(ext_rows, ext_cols, -1)).reshape(
        -1, WIN * WIN, 3, HEADS, width_model // HEADS
    )
    row_global = row_anchor - shift_size + jnp.arange(ext_rows, dtype=jnp.int32)
    col_global = col_anchor - shift_size + jnp.arange(ext_cols, dtype=jnp.int32)
    row_wrap = ((row_global < 0) | (row_global >= grid_rows)).astype(jnp.int32)
    col_wrap = ((col_global < 0) | (col_global >= grid_cols)).astype(jnp.int32)
    labels = to_windows((2 * row_wrap[:, None] + col_wrap[None, :])[:, :, None])[:, :, 0]
    mixed = from_windows(attend(joint, labels, relative_bias), ext_rows, ext_cols)
    own_mixed = mixed[
        shift_size : shift_size + tile_rows, shift_size : shift_size + tile_cols
    ].reshape(-1, width_model)
    residual = tokens.reshape(-1, width_model).astype(jnp.float32) + jnp.dot(
        own_mixed, merge_weight, preferred_element_type=jnp.float32
    )
    normed_second = layer_norm(residual, second_gain).astype(jnp.bfloat16)
    hidden = jax.nn.gelu(
        jnp.dot(normed_second, expand_weight, preferred_element_type=jnp.float32)
    ).astype(jnp.bfloat16)
    block_out = (
        residual + jnp.dot(hidden, shrink_weight, preferred_element_type=jnp.float32)
    ).astype(jnp.bfloat16)
    features = jnp.dot(block_out, lateral_weight, preferred_element_type=jnp.float32).astype(
        jnp.bfloat16
    )
    features = features.reshape(tile_rows, tile_cols, -1)
    geometry = box_geometry.reshape(-1, 4)
    capacity = geometry.shape[0]
    tile_count = box_counts.reshape(())
    owner_list = box_owner.reshape(-1)
    targets = soft_target.reshape(capacity, -1)
    slot_range = jnp.arange(capacity, dtype=jnp.int32)
    is_valid = slot_range < tile_count
    tgt = targets.reshape(capacity, CROP, CROP).transpose(2, 0, 1).reshape(ROWS, CROP)
    tgt = jnp.pad(tgt.astype(jnp.float32), ((0, 0), (0, 128 - CROP)))
    feature_grad, local_logits = mask_head(
        7, geometry, box_counts, features, conv_weight, mask_weight.reshape(1, -1), tgt
    )
    local_logits = local_logits[:, :CROP].reshape(CROP, capacity, CROP).transpose(1, 2, 0)
    owner_count = lax.axis_size("row")
    routing = (
        owner_list[None, :] == jnp.arange(owner_count, dtype=jnp.int32)[:, None]
    ) & is_valid[None, :]
    routing = routing.astype(jnp.float32)
    payload = jnp.concatenate(
        [local_logits.reshape(capacity, -1), jnp.ones((capacity, 60), jnp.float32)], axis=1
    )
    outgoing = jnp.dot(routing, payload, precision=lax.Precision.HIGHEST)
    arriving = lax.all_to_all(outgoing, "row", split_axis=0, concat_axis=0, tiled=True)
    picker = compact_order(arriving[:, -1] > 0.5)
    logits = jnp.dot(
        picker.astype(jnp.float32), arriving[:, : CROP * CROP], precision=lax.Precision.HIGHEST
    )
    mask_logits = logits.reshape(1, 1, BOX_OWN, -1)
    return (features, feature_grad, mask_logits)


def solution(mesh):
    placed = (
        P("row", "col", None),
        P(),
        P(),
        P(),
        P(),
        P(),
        P(),
        P(),
        P(),
        P(),
        P(),
        P("row", "col", None, None),
        P("row", "col"),
        P("row", "col", None),
        P("row", "col", None, None),
    )
    return jax.shard_map(
        shards,
        mesh=mesh,
        in_specs=placed,
        out_specs=(P("row", "col", None), P("row", "col", None), P("row", "col", None, None)),
        check_vma=False,
    )
```

```python
import functools
import jax
import jax.numpy as jnp
from jax import lax
from jax.experimental import pallas as pl
from jax.experimental.pallas import tpu as pltpu
from jax.sharding import PartitionSpec as P

CROP = 14
BOX_OWN = 8
EPSILON = 1e-05
G1 = 0.7978845608028654
G2 = G1 * 0.044715
ROWS = 224
MESH = pl.DeviceIdType.MESH


def norm_rows(x, gain):
    x = x - jnp.mean(x, axis=-1, keepdims=True)
    return x * lax.rsqrt(jnp.mean(x * x, axis=-1, keepdims=True) + EPSILON) * gain


def neighbours():
    row_at, row_n = lax.axis_index("row"), lax.axis_size("row")
    col_at, col_n = lax.axis_index("col"), lax.axis_size("col")
    found = []
    for dr in (-1, 0, 1):
        for dc in (-1, 0, 1):
            if dr == 0 and dc == 0:
                continue
            there = None
            for d, at, n in ((dr, row_at, row_n), (dc, col_at, col_n)):
                if d:
                    ok = at > 0 if d < 0 else at < n - 1
                    there = ok if there is None else there & ok
            found.append((dr, dc, there, (row_at + dr, col_at + dc)))
    return found


def swin_kernel(
    tok, cols, g1, g2, wj_h, wm_h, we_h, ws_h, rb_h, wl_h, out,
    wj, wm, we, ws, rb, wl, E, J, ME, BB, ON,
    top, bottom, left, right, corner, send_sem, recv_sem, load_sem,
):
    f32, bf16 = jnp.float32, jnp.bfloat16
    row_at, row_n = lax.axis_index("row"), lax.axis_size("row")
    col_at, col_n = lax.axis_index("col"), lax.axis_size("col")
    loads = [
        pltpu.make_async_copy(src, dst, load_sem.at[n])
        for n, (src, dst) in enumerate(
            ((wj_h, wj), (rb_h, rb), (wm_h, wm), (we_h, we), (ws_h, ws), (wl_h, wl))
        )
    ]
    for load in loads:
        load.start()
    around = neighbours()
    barrier = pltpu.get_barrier_semaphore()
    for dr, dc, there, peer in around:

        @pl.when(there)
        def _(peer=peer):
            pl.semaphore_signal(barrier, inc=1, device_id=peer, device_id_type=MESH)

    near_rows = jnp.where(row_at > 0, 1, 0) + jnp.where(row_at < row_n - 1, 1, 0) + 1
    near_cols = jnp.where(col_at > 0, 1, 0) + jnp.where(col_at < col_n - 1, 1, 0) + 1
    pl.semaphore_wait(barrier, near_rows * near_cols - 1)

    def parts(dr, dc):
        if dc == 0:
            return (tok.at[0:4], bottom) if dr < 0 else (tok.at[28:32], top)
        side = cols.at[0] if dc < 0 else cols.at[1]
        if dr == 0:
            return (side, right) if dc < 0 else (side, left)
        piece = side.at[0:16] if dr < 0 else side.at[112:128]
        return piece, corner.at[(0 if dr > 0 else 2) + (0 if dc > 0 else 1)]

    def copy_to(n, dr, dc, peer):
        src, dst = parts(dr, dc)
        return pltpu.make_async_remote_copy(
            src_ref=src, dst_ref=dst, send_sem=send_sem.at[n], recv_sem=recv_sem.at[n],
            device_id=peer, device_id_type=MESH,
        )

    for n, (dr, dc, there, peer) in enumerate(around):

        @pl.when(there)
        def _(n=n, dr=dr, dc=dc, peer=peer):
            copy_to(n, dr, dc, peer).start()

    def fill(r, carry):
        E[r + 4, 4:36, :] = tok[r].astype(f32)
        return carry

    lax.fori_loop(0, 32, fill, 0)
    loads[0].wait()
    loads[1].wait()
    for c in range(6):
        BB[c] = jnp.concatenate([rb[2 * c], rb[2 * c + 1]], axis=1)
    lane = lax.broadcasted_iota(jnp.int32, (64, 128), 1)
    head_of = lane // 32
    zero = jnp.zeros((64, 128), bf16)
    for h in range(4):
        ON[h * 64 : (h + 1) * 64] = jnp.where(head_of == h, 1.0, 0.0).astype(bf16)
    low = lane < 64
    qi = lax.broadcasted_iota(jnp.int32, (64, 128), 0)
    kj = lane % 64
    row_cut = (qi // 32) != (kj // 32)
    col_cut = ((qi // 4) % 2) != ((kj // 4) % 2)

    def windows(wi, across):
        first, last = across[0], across[-1]
        count = len(across)
        if count == last - first + 1:
            x = E[pl.ds(wi * 8, 8), first * 8 : (last + 1) * 8, :]
        else:
            x = jnp.concatenate([E[pl.ds(wi * 8, 8), j * 8 : (j + 1) * 8, :] for j in across], axis=1)
        x = norm_rows(x, g1[...].reshape(1, 1, 384))
        m = jnp.concatenate(
            [x[:, n * 8 : (n + 1) * 8, :].reshape(64, 384) for n in range(count)], axis=0
        ).astype(bf16)
        top_row = count * 64
        J[0:top_row, 0:384] = (
            jnp.dot(m, wj[:, 0:384], preferred_element_type=f32) * 32**-0.5
        ).astype(bf16)
        J[0:top_row, 384:1152] = jnp.dot(m, wj[:, 384:1152], preferred_element_type=f32).astype(bf16)
        row_flag = ((wi == 0) & (row_at == 0)) | ((wi == 4) & (row_at == row_n - 1))
        for n, j in enumerate(across):
            cut = row_cut & row_flag
            if j == 0:
                cut = cut | (col_cut & (col_at == 0))
            if j == 4:
                cut = cut | (col_cut & (col_at == col_n - 1))
            sl = slice(n * 64, (n + 1) * 64)
            for g in range(3):
                q = J[sl, g * 128 : (g + 1) * 128]
                k = J[sl, 384 + g * 128 : 384 + (g + 1) * 128]
                v = J[sl, 768 + g * 128 : 768 + (g + 1) * 128]
                kb = jnp.concatenate([jnp.where(head_of == h, k, zero) for h in range(4)], axis=0)
                s = lax.dot_general(q, kb, (((1,), (1,)), ((), ())), preferred_element_type=f32)
                es = []
                for c in range(2):
                    b = s[:, c * 128 : (c + 1) * 128] + BB[2 * g + c]
                    b = jnp.where(cut, -1e9, b)
                    m0 = jnp.max(jnp.where(low, b, -3e38), axis=1, keepdims=True)
                    m1 = jnp.max(jnp.where(low, -3e38, b), axis=1, keepdims=True)
                    es.append(jnp.exp(b - jnp.where(low, m0, m1)).astype(bf16))
                p = jnp.concatenate(es, axis=1)
                vb = jnp.concatenate([jnp.where(head_of == h, v, zero) for h in range(4)], axis=0)
                o = jnp.dot(p, jnp.concatenate([vb, ON[...]], axis=1), preferred_element_type=f32)
                o = o[:, 0:128] / o[:, 128:256]
                ME[pl.ds(wi * 8, 8), j * 8 : (j + 1) * 8, g * 128 : (g + 1) * 128] = o.reshape(8, 8, 128)

    def inner(n, carry):
        windows(n + 1, (1, 2, 3))
        return carry

    lax.fori_loop(0, 3, inner, 0)

    def land(dr, dc):
        rows = 0 if dr < 0 else 36
        if dc == 0:
            src = top if dr < 0 else bottom
            for r in range(4):
                yield (rows + r, slice(4, 36), lambda r=r: src[r].astype(f32))
            return
        span = slice(0, 4) if dc < 0 else slice(36, 40)
        if dr == 0:
            src = left if dc < 0 else right
            for h in range(8):
                for r in range(4):
                    yield (
                        4 + h * 4 + r, span,
                        lambda h=h, r=r: src[h * 16 : (h + 1) * 16].astype(f32)[r * 4 : (r + 1) * 4],
                    )
            return
        piece = corner.at[(0 if dr < 0 else 2) + (0 if dc < 0 else 1)]
        for r in range(4):
            yield (rows + r, span, lambda r=r: piece[...].astype(f32)[r * 4 : (r + 1) * 4])

    for n, (dr, dc, there, peer) in enumerate(around):

        @pl.when(there)
        def _(n=n, dr=dr, dc=dc, peer=peer):
            copy_to(n, dr, dc, peer).wait_send()
            copy_to(len(around) - 1 - n, -dr, -dc, peer).wait_recv()
            for r, span, value in land(dr, dc):
                E[r, span, :] = value()

        @pl.when(jnp.logical_not(there))
        def _(dr=dr, dc=dc):
            for r, span, value in land(dr, dc):
                E[r, span, :] = jnp.zeros((span.stop - span.start, 384), f32)

    def sides(n, carry):
        windows(n + 1, (0, 4))
        return carry

    lax.fori_loop(0, 3, sides, 0)

    def ends(n, carry):
        windows(n * 4, (0, 1, 2, 3, 4))
        return carry

    lax.fori_loop(0, 2, ends, 0)
    for load in loads[2:]:
        load.wait()
    R = 16

    def tail(c, carry):
        r0 = c * R
        mixed = jnp.concatenate([ME[r0 + q + 4, 4:36, :] for q in range(R)], axis=0).astype(bf16)
        t = jnp.concatenate([tok[r0 + q] for q in range(R)], axis=0).astype(f32)
        res = t + jnp.dot(mixed, wm[...], preferred_element_type=f32)
        n2 = norm_rows(res, g2[...].reshape(1, 384)).astype(bf16)
        h = jnp.dot(n2, we[...], preferred_element_type=f32)
        h = (h * (0.5 + 0.5 * jnp.tanh(h * (G1 + G2 * (h * h))))).astype(bf16)
        b = (res + jnp.dot(h, ws[...], preferred_element_type=f32)).astype(bf16)
        f = jnp.dot(b, wl[...], preferred_element_type=f32).astype(bf16)
        for q in range(R):
            out[r0 + q] = f[q * 32 : (q + 1) * 32]
        return carry

    lax.fori_loop(0, 32 // R, tail, 0)


def swin(tok, cols, g1, g2, wj, wm, we, ws, rb, wl):
    V = pl.BlockSpec(memory_space=pltpu.VMEM)
    A = pl.BlockSpec(memory_space=pl.ANY)
    weights = (wj, wm, we, ws, rb, wl)
    return pl.pallas_call(
        swin_kernel,
        out_shape=jax.ShapeDtypeStruct((32, 32, 256), jnp.bfloat16),
        in_specs=[V] * 4 + [A] * 6,
        out_specs=V,
        scratch_shapes=[pltpu.VMEM(w.shape, w.dtype) for w in weights]
        + [
            pltpu.VMEM((40, 40, 384), jnp.float32),
            pltpu.VMEM((320, 1152), jnp.bfloat16),
            pltpu.VMEM((40, 40, 384), jnp.float32),
            pltpu.VMEM((6, 64, 128), jnp.float32),
            pltpu.VMEM((256, 128), jnp.bfloat16),
            pltpu.VMEM((4, 32, 384), jnp.bfloat16),
            pltpu.VMEM((4, 32, 384), jnp.bfloat16),
            pltpu.VMEM((128, 384), jnp.bfloat16),
            pltpu.VMEM((128, 384), jnp.bfloat16),
            pltpu.VMEM((4, 16, 384), jnp.bfloat16),
            pltpu.SemaphoreType.DMA((8,)),
            pltpu.SemaphoreType.DMA((8,)),
            pltpu.SemaphoreType.DMA((6,)),
        ],
        compiler_params=pltpu.CompilerParams(
            vmem_limit_bytes=63 << 20, collective_id=0, has_side_effects=True
        ),
    )(tok, cols, g1, g2, wj, wm, we, ws, rb, wl)


def gelu_pair(x):
    x2 = x * x
    inner = x * (G1 + (G2) * x2)
    th = jnp.tanh(inner)
    half = 0.5 + 0.5 * th
    act = x * half
    slope = half + (0.5 * x) * (1.0 - th * th) * (G1 + (3.0 * G2) * x2)
    return act, slope

def mask_kernel(U, gs, cs, geom, own, soft, feat, w_h, mw, fg, rt, feat_out, X, Y, D, tgt, lg, w, sem):
    f32, bf16 = jnp.float32, jnp.bfloat16
    cnt = cs[0, 0]
    loads = [pltpu.make_async_copy(w_h.at[n], w.at[n], sem.at[n]) for n in range(4)]
    for load in loads:
        load.start()
    store = pltpu.make_async_copy(feat, feat_out, sem.at[4])
    store.start()
    zrow = jnp.zeros((256, 256), bf16)
    for B in (X, Y):
        B[0] = zrow
        B[15] = zrow
        for u in range(1, 15):
            B[u, 0:16, :] = zrow[0:16]
            B[u, 240:256, :] = zrow[0:16]
    g = geom[0, 0]
    valid = lax.broadcasted_iota(jnp.int32, (16, 1), 0) < cnt
    rep = lambda col: jnp.concatenate([col] * 14, axis=0)
    lefts, widths = rep(g[:, 1:2]), rep(g[:, 3:4])
    heights = rep(jnp.where(valid, g[:, 2:3], 0))
    row = lax.broadcasted_iota(jnp.int32, (ROWS, 1), 0)
    vv, kk = row // 16, row % 16
    target = jnp.where(vv < widths, kk * 32 + lefts + vv, -1)
    lane = lax.broadcasted_iota(jnp.int32, (ROWS, 512), 1)
    pick = jnp.where(lane == target, 1.0, 0.0).astype(bf16)
    in_w = vv < widths

    soft_rows = soft[0, 0]
    cell = lax.broadcasted_iota(jnp.int32, (CROP * CROP, 128), 0)
    step = lax.broadcasted_iota(jnp.int32, (CROP * CROP, 128), 1)
    for v in range(CROP):
        spread = jnp.where(cell == step * CROP + v, 1.0, 0.0).astype(bf16)
        tgt[v * 16:(v + 1) * 16] = jnp.dot(soft_rows, spread, preferred_element_type=f32)

    def gather(u, c):
        strips = jnp.concatenate([feat[gs[0, 0, k, 0] + u] for k in range(16)], axis=0)
        crop = jnp.dot(pick, strips, preferred_element_type=f32)
        crop = jnp.where(u < heights, crop, 0.0)
        X[u + 1, 16:240, :] = crop.astype(bf16)
        return c
    lax.fori_loop(0, 14, gather, 0)

    def fwd(src, dst, l):
        loads[l].wait()
        def body(i, c):
            u0 = i * U
            cols = []
            for s in range(3):
                for t in range(3):
                    cols.append(jnp.concatenate([src[u0 + q + s, t * 16:t * 16 + ROWS, :] for q in range(U)], axis=0))
            pre = jnp.dot(jnp.concatenate(cols, axis=1), w[l], preferred_element_type=f32)
            act, slope = gelu_pair(pre)
            for q in range(U):
                a = act[q * ROWS:(q + 1) * ROWS].astype(bf16)
                sl = slope[q * ROWS:(q + 1) * ROWS]
                if l < 3:
                    dst[u0 + q + 1, 16:240, :] = a
                    D[l, u0 + q] = sl.astype(bf16)
                else:
                    u = u0 + q
                    m = mw[...].astype(f32).reshape(1, 256)
                    logit = jnp.sum(a.astype(f32) * m, axis=1, keepdims=True)
                    sel = lax.broadcasted_iota(jnp.int32, (ROWS, 128), 1) == u
                    lg[...] = jnp.where(sel, logit, lg[...])
                    tg = jnp.sum(jnp.where(sel, tgt[...], 0.0), axis=1, keepdims=True)
                    gl = jnp.where(in_w & (u < heights), 128.0 * (jax.nn.sigmoid(logit) - tg), 0.0)
                    dst[u + 1, 16:240, :] = (gl * m * sl).astype(bf16)
            return c
        lax.fori_loop(0, 14 // U, body, 0)

    lg[...] = jnp.zeros_like(lg)
    fwd(X, Y, 0)
    fwd(Y, X, 1)
    fwd(X, Y, 2)
    fwd(Y, X, 3)

    spot = lax.broadcasted_iota(jnp.int32, (128, 256), 1)
    from_u = lax.broadcasted_iota(jnp.int32, (128, 256), 0)

    def halves(a):
        hi = a.astype(bf16)
        return hi, (a - hi.astype(f32)).astype(bf16)

    flat = jnp.zeros((16, 256), f32)
    for v in range(CROP):
        spread = jnp.where((spot == from_u * CROP + v) & (from_u < CROP), 1.0, 0.0).astype(bf16)
        for part in halves(lg[v * 16:(v + 1) * 16]):
            flat = flat + jnp.dot(part, spread, preferred_element_type=f32)
    flat = jnp.where(lax.broadcasted_iota(jnp.int32, (16, 256), 1) < CROP * CROP, flat, 1.0)
    used = lax.broadcasted_iota(jnp.int32, (16, 16), 1) < cnt
    sent = jnp.where((own[0] == lax.broadcasted_iota(jnp.int32, (16, 16), 0)) & used, 1.0, 0.0).astype(bf16)
    routed = jnp.zeros((16, 256), f32)
    for part in halves(flat):
        routed = routed + jnp.dot(sent, part, preferred_element_type=f32)
    for o in range(16):
        rt[o] = routed[o:o + 1]

    fg[...] = jnp.zeros_like(fg)

    def bwd(src, dst, l):
        def body(i, c):
            u0 = i * U
            acc = None
            for s in range(3):
                for t in range(3):
                    a = jnp.concatenate([src[u0 + q + 2 - s, (2 - t) * 16:(2 - t) * 16 + ROWS, :] for q in range(U)], axis=0)
                    tap = 3 * s + t
                    d = lax.dot_general(a, w[l, tap * 256:(tap + 1) * 256, :], (((1,), (1,)), ((), ())), preferred_element_type=f32)
                    acc = d if acc is None else acc + d
            for q in range(U):
                gq = acc[q * ROWS:(q + 1) * ROWS]
                if l > 0:
                    dst[u0 + q + 1, 16:240, :] = (gq * D[l - 1, u0 + q].astype(f32)).astype(bf16)
                else:
                    u = u0 + q
                    gq = jnp.where(u < heights, gq, 0.0).astype(bf16)
                    z = lax.dot_general(pick, gq, (((0,), (0,)), ((), ())), preferred_element_type=f32)
                    for k in range(16):
                        fg[gs[0, 0, k, 0] + u] += z[k * 32:(k + 1) * 32]
            return c
        lax.fori_loop(0, 14 // U, body, 0)
    bwd(X, Y, 3)
    bwd(Y, X, 2)
    bwd(X, Y, 1)
    bwd(Y, X, 0)
    store.wait()

def mask_head(geometry, count, owner, soft, feat, conv_w, mask_w):
    V = pl.BlockSpec(memory_space=pltpu.VMEM)
    S = pl.BlockSpec(memory_space=pltpu.SMEM)
    A = pl.BlockSpec(memory_space=pl.ANY)
    return pl.pallas_call(
        functools.partial(mask_kernel, 7),
        out_shape=(
            jax.ShapeDtypeStruct((32, 32, 256), jnp.float32),
            jax.ShapeDtypeStruct((16, 1, 256), jnp.float32),
            jax.ShapeDtypeStruct((32, 32, 256), jnp.bfloat16),
        ),
        in_specs=[S, S, V, V, V, V, A, V],
        out_specs=(V, V, A),
        scratch_shapes=[
            pltpu.VMEM((16, 256, 256), jnp.bfloat16),
            pltpu.VMEM((16, 256, 256), jnp.bfloat16),
            pltpu.VMEM((3, 14, ROWS, 256), jnp.bfloat16),
            pltpu.VMEM((ROWS, 128), jnp.float32),
            pltpu.VMEM((ROWS, 128), jnp.float32),
            pltpu.VMEM((4, 2304, 256), jnp.bfloat16),
            pltpu.SemaphoreType.DMA((5,)),
        ],
        compiler_params=pltpu.CompilerParams(vmem_limit_bytes=63 << 20),
    )(geometry, count, geometry, owner, soft, feat, conv_w, mask_w)


def deal_kernel(outgoing, out, recv, send_sem, recv_sem):
    me, n = lax.axis_index("row"), lax.axis_size("row")
    col = lax.axis_index("col")
    barrier = pltpu.get_barrier_semaphore()
    for d in range(1, 16):
        pl.semaphore_signal(
            barrier, inc=1, device_id=(lax.rem(me + d, n), col), device_id_type=MESH
        )
    pl.semaphore_wait(barrier, 15)

    def copy_to(d, slot):
        peer = lax.rem(me + d, n)
        return pltpu.make_async_remote_copy(
            src_ref=outgoing.at[peer], dst_ref=recv.at[slot],
            send_sem=send_sem.at[d], recv_sem=recv_sem.at[d],
            device_id=(peer, col), device_id_type=MESH,
        )

    for d in range(1, 16):
        copy_to(d, me).start()
    recv[me] = outgoing[me]
    for d in range(1, 16):
        copy_to(d, lax.rem(me + n - d, n)).wait()
    got = jnp.concatenate([recv[i] for i in range(16)], axis=0)
    flag = jnp.where(got[:, 255:256] > 0.5, 1.0, 0.0)
    later = lax.broadcasted_iota(jnp.int32, (16, 16), 0) > lax.broadcasted_iota(
        jnp.int32, (16, 16), 1
    )
    place = jnp.dot(
        jnp.where(later, 1.0, 0.0).astype(jnp.bfloat16),
        jnp.broadcast_to(flag, (16, 128)).astype(jnp.bfloat16),
        preferred_element_type=jnp.float32,
    )[:, 0:1]
    rows = [
        jnp.sum(jnp.where((place == float(i)) & (flag > 0.5), got, 0.0), axis=0, keepdims=True)
        for i in range(BOX_OWN)
    ]
    out[0, 0] = jnp.concatenate(rows, axis=0)[:, 0 : CROP * CROP]


def deal_logits(outgoing):
    V = pl.BlockSpec(memory_space=pltpu.VMEM)
    return pl.pallas_call(
        deal_kernel,
        out_shape=jax.ShapeDtypeStruct((1, 1, BOX_OWN, CROP * CROP), jnp.float32),
        in_specs=[V],
        out_specs=V,
        scratch_shapes=[
            pltpu.VMEM((16, 1, 256), jnp.float32),
            pltpu.SemaphoreType.DMA((16,)),
            pltpu.SemaphoreType.DMA((16,)),
        ],
        compiler_params=pltpu.CompilerParams(collective_id=1, has_side_effects=True),
    )(outgoing)


def shards(
    tokens,
    first_gain,
    second_gain,
    joint_weight,
    merge_weight,
    expand_weight,
    shrink_weight,
    relative_bias,
    lateral_weight,
    conv_weight,
    mask_weight,
    box_geometry,
    box_counts,
    box_owner,
    soft_target,
):
    cols = jnp.stack([tokens[:, :4].reshape(128, -1), tokens[:, 28:].reshape(128, -1)])
    features = swin(
        tokens, cols, first_gain, second_gain, joint_weight, merge_weight,
        expand_weight, shrink_weight, relative_bias, lateral_weight,
    )
    feature_grad, outgoing, features = mask_head(
        box_geometry, box_counts, box_owner, soft_target, features, conv_weight, mask_weight
    )
    return (features, feature_grad, deal_logits(outgoing))


def solution(mesh):
    placed = (
        P("row", "col", None),
        P(),
        P(),
        P(),
        P(),
        P(),
        P(),
        P(),
        P(),
        P(),
        P(),
        P("row", "col", None, None),
        P("row", "col"),
        P("row", "col", None),
        P("row", "col", None, None),
    )
    return jax.shard_map(
        shards,
        mesh=mesh,
        in_specs=placed,
        out_specs=(P("row", "col", None), P("row", "col", None), P("row", "col", None, None)),
        check_vma=False,
    )
```

```python
import functools
import jax
import jax.numpy as jnp
from jax import lax
from jax.experimental import pallas as pl
from jax.experimental.pallas import tpu as pltpu
from jax.sharding import PartitionSpec as P

CROP = 14
BOX_OWN = 8
EPSILON = 1e-05
G1 = 0.7978845608028654
G2 = G1 * 0.044715
ROWS = 224
MESH = pl.DeviceIdType.MESH


def norm_rows(x, gain):
    x = x - jnp.mean(x, axis=-1, keepdims=True)
    return x * lax.rsqrt(jnp.mean(x * x, axis=-1, keepdims=True) + EPSILON) * gain


def neighbours():
    row_at, row_n = lax.axis_index("row"), lax.axis_size("row")
    col_at, col_n = lax.axis_index("col"), lax.axis_size("col")
    found = []
    for dr in (-1, 0, 1):
        for dc in (-1, 0, 1):
            if dr == 0 and dc == 0:
                continue
            there = None
            for d, at, n in ((dr, row_at, row_n), (dc, col_at, col_n)):
                if d:
                    ok = at > 0 if d < 0 else at < n - 1
                    there = ok if there is None else there & ok
            found.append((dr, dc, there, (row_at + dr, col_at + dc)))
    return found


def swin_kernel(
    tok, g1, g2, wj_h, wm_h, we_h, ws_h, rb_h, wl_h, out,
    wj, wm, we, ws, rb, wl, E, J, ME, BB, ON,
    top, bottom, left, right, corner, send_sem, recv_sem, load_sem,
):
    f32, bf16 = jnp.float32, jnp.bfloat16
    row_at, row_n = lax.axis_index("row"), lax.axis_size("row")
    col_at, col_n = lax.axis_index("col"), lax.axis_size("col")
    loads = [
        pltpu.make_async_copy(src, dst, load_sem.at[n])
        for n, (src, dst) in enumerate(
            ((wj_h, wj), (rb_h, rb), (wm_h, wm), (we_h, we), (ws_h, ws), (wl_h, wl))
        )
    ]
    for load in loads:
        load.start()
    around = neighbours()
    barrier = pltpu.get_barrier_semaphore()
    for dr, dc, there, peer in around:

        @pl.when(there)
        def _(peer=peer):
            pl.semaphore_signal(barrier, inc=1, device_id=peer, device_id_type=MESH)

    near_rows = jnp.where(row_at > 0, 1, 0) + jnp.where(row_at < row_n - 1, 1, 0) + 1
    near_cols = jnp.where(col_at > 0, 1, 0) + jnp.where(col_at < col_n - 1, 1, 0) + 1
    pl.semaphore_wait(barrier, near_rows * near_cols - 1)

    def parts(dr, dc):
        if dc == 0:
            return (tok.at[0:4], bottom) if dr < 0 else (tok.at[28:32], top)
        span = slice(0, 8) if dc < 0 else slice(24, 32)
        if dr == 0:
            return tok.at[:, span], (right if dc < 0 else left)
        piece = tok.at[0:4, span] if dr < 0 else tok.at[28:32, span]
        return piece, corner.at[(0 if dr > 0 else 2) + (0 if dc > 0 else 1)]

    def copy_to(n, dr, dc, peer):
        src, dst = parts(dr, dc)
        return pltpu.make_async_remote_copy(
            src_ref=src, dst_ref=dst, send_sem=send_sem.at[n], recv_sem=recv_sem.at[n],
            device_id=peer, device_id_type=MESH,
        )

    for n, (dr, dc, there, peer) in enumerate(around):

        @pl.when(there)
        def _(n=n, dr=dr, dc=dc, peer=peer):
            copy_to(n, dr, dc, peer).start()

    def fill(r, carry):
        E[r + 4, 4:36, :] = tok[r].astype(f32)
        return carry

    lax.fori_loop(0, 32, fill, 0)
    loads[0].wait()
    loads[1].wait()
    for c in range(6):
        BB[c] = jnp.concatenate([rb[2 * c], rb[2 * c + 1]], axis=1)
    lane = lax.broadcasted_iota(jnp.int32, (64, 128), 1)
    head_of = lane // 32
    zero = jnp.zeros((64, 128), bf16)
    for h in range(4):
        ON[h * 64 : (h + 1) * 64] = jnp.where(head_of == h, 1.0, 0.0).astype(bf16)
    low = lane < 64
    qi = lax.broadcasted_iota(jnp.int32, (64, 128), 0)
    kj = lane % 64
    row_cut = (qi // 32) != (kj // 32)
    col_cut = ((qi // 4) % 2) != ((kj // 4) % 2)

    def windows(wi, across):
        first, last = across[0], across[-1]
        count = len(across)
        if count == last - first + 1:
            x = E[pl.ds(wi * 8, 8), first * 8 : (last + 1) * 8, :]
        else:
            x = jnp.concatenate([E[pl.ds(wi * 8, 8), j * 8 : (j + 1) * 8, :] for j in across], axis=1)
        x = norm_rows(x, g1[...].reshape(1, 1, 384))
        m = jnp.concatenate(
            [x[:, n * 8 : (n + 1) * 8, :].reshape(64, 384) for n in range(count)], axis=0
        ).astype(bf16)
        top_row = count * 64
        J[0:top_row, 0:384] = (
            jnp.dot(m, wj[:, 0:384], preferred_element_type=f32) * 32**-0.5
        ).astype(bf16)
        J[0:top_row, 384:1152] = jnp.dot(m, wj[:, 384:1152], preferred_element_type=f32).astype(bf16)
        row_flag = ((wi == 0) & (row_at == 0)) | ((wi == 4) & (row_at == row_n - 1))
        for n, j in enumerate(across):
            cut = row_cut & row_flag
            if j == 0:
                cut = cut | (col_cut & (col_at == 0))
            if j == 4:
                cut = cut | (col_cut & (col_at == col_n - 1))
            sl = slice(n * 64, (n + 1) * 64)
            for g in range(3):
                q = J[sl, g * 128 : (g + 1) * 128]
                k = J[sl, 384 + g * 128 : 384 + (g + 1) * 128]
                v = J[sl, 768 + g * 128 : 768 + (g + 1) * 128]
                kb = jnp.concatenate([jnp.where(head_of == h, k, zero) for h in range(4)], axis=0)
                s = lax.dot_general(q, kb, (((1,), (1,)), ((), ())), preferred_element_type=f32)
                es = []
                for c in range(2):
                    b = s[:, c * 128 : (c + 1) * 128] + BB[2 * g + c]
                    b = jnp.where(cut, -1e9, b)
                    m0 = jnp.max(jnp.where(low, b, -3e38), axis=1, keepdims=True)
                    m1 = jnp.max(jnp.where(low, -3e38, b), axis=1, keepdims=True)
                    es.append(jnp.exp(b - jnp.where(low, m0, m1)).astype(bf16))
                p = jnp.concatenate(es, axis=1)
                vb = jnp.concatenate([jnp.where(head_of == h, v, zero) for h in range(4)], axis=0)
                o = jnp.dot(p, jnp.concatenate([vb, ON[...]], axis=1), preferred_element_type=f32)
                o = o[:, 0:128] / o[:, 128:256]
                ME[pl.ds(wi * 8, 8), j * 8 : (j + 1) * 8, g * 128 : (g + 1) * 128] = o.reshape(8, 8, 128)

    def inner(n, carry):
        windows(n + 1, (1, 2, 3))
        return carry

    lax.fori_loop(0, 3, inner, 0)

    def land(dr, dc):
        rows = 0 if dr < 0 else 36
        if dc == 0:
            src = top if dr < 0 else bottom
            for r in range(4):
                yield (rows + r, slice(4, 36), lambda r=r: src[r].astype(f32))
            return
        span, part = (slice(0, 4), slice(4, 8)) if dc < 0 else (slice(36, 40), slice(0, 4))
        if dr == 0:
            src = left if dc < 0 else right
            for r in range(32):
                yield (4 + r, span, lambda r=r: src[r].astype(f32)[part])
            return
        piece = corner.at[(0 if dr < 0 else 2) + (0 if dc < 0 else 1)]
        for r in range(4):
            yield (rows + r, span, lambda r=r: piece[r].astype(f32)[part])

    for n, (dr, dc, there, peer) in enumerate(around):

        @pl.when(there)
        def _(n=n, dr=dr, dc=dc, peer=peer):
            copy_to(n, dr, dc, peer).wait_send()
            copy_to(len(around) - 1 - n, -dr, -dc, peer).wait_recv()
            for r, span, value in land(dr, dc):
                E[r, span, :] = value()

        @pl.when(jnp.logical_not(there))
        def _(dr=dr, dc=dc):
            for r, span, value in land(dr, dc):
                E[r, span, :] = jnp.zeros((span.stop - span.start, 384), f32)

    def sides(n, carry):
        windows(n + 1, (0, 4))
        return carry

    lax.fori_loop(0, 3, sides, 0)

    def ends(n, carry):
        windows(n * 4, (0, 1, 2, 3, 4))
        return carry

    lax.fori_loop(0, 2, ends, 0)
    for load in loads[2:]:
        load.wait()
    R = 16

    def tail(c, carry):
        r0 = c * R
        mixed = jnp.concatenate([ME[r0 + q + 4, 4:36, :] for q in range(R)], axis=0).astype(bf16)
        t = jnp.concatenate([tok[r0 + q] for q in range(R)], axis=0).astype(f32)
        res = t + jnp.dot(mixed, wm[...], preferred_element_type=f32)
        n2 = norm_rows(res, g2[...].reshape(1, 384)).astype(bf16)
        h = jnp.dot(n2, we[...], preferred_element_type=f32)
        h = (h * (0.5 + 0.5 * jnp.tanh(h * (G1 + G2 * (h * h))))).astype(bf16)
        b = (res + jnp.dot(h, ws[...], preferred_element_type=f32)).astype(bf16)
        f = jnp.dot(b, wl[...], preferred_element_type=f32).astype(bf16)
        for q in range(R):
            out[r0 + q] = f[q * 32 : (q + 1) * 32]
        return carry

    lax.fori_loop(0, 32 // R, tail, 0)


def swin(tok, g1, g2, wj, wm, we, ws, rb, wl):
    V = pl.BlockSpec(memory_space=pltpu.VMEM)
    A = pl.BlockSpec(memory_space=pl.ANY)
    weights = (wj, wm, we, ws, rb, wl)
    return pl.pallas_call(
        swin_kernel,
        out_shape=jax.ShapeDtypeStruct((32, 32, 256), jnp.bfloat16),
        in_specs=[V] * 3 + [A] * 6,
        out_specs=V,
        scratch_shapes=[pltpu.VMEM(w.shape, w.dtype) for w in weights]
        + [
            pltpu.VMEM((40, 40, 384), jnp.float32),
            pltpu.VMEM((320, 1152), jnp.bfloat16),
            pltpu.VMEM((40, 40, 384), jnp.float32),
            pltpu.VMEM((6, 64, 128), jnp.float32),
            pltpu.VMEM((256, 128), jnp.bfloat16),
            pltpu.VMEM((4, 32, 384), jnp.bfloat16),
            pltpu.VMEM((4, 32, 384), jnp.bfloat16),
            pltpu.VMEM((32, 8, 384), jnp.bfloat16),
            pltpu.VMEM((32, 8, 384), jnp.bfloat16),
            pltpu.VMEM((4, 4, 8, 384), jnp.bfloat16),
            pltpu.SemaphoreType.DMA((8,)),
            pltpu.SemaphoreType.DMA((8,)),
            pltpu.SemaphoreType.DMA((6,)),
        ],
        compiler_params=pltpu.CompilerParams(
            vmem_limit_bytes=63 << 20, collective_id=0, has_side_effects=True
        ),
    )(tok, g1, g2, wj, wm, we, ws, rb, wl)


def gelu_pair(x):
    x2 = x * x
    half = 0.5 + 0.5 * jnp.tanh(x * (G1 + G2 * x2))
    act = x * half
    slope = half + act * (1.0 - half) * (2.0 * G1 + (6.0 * G2) * x2)
    return act, slope


def halves(a):
    hi = a.astype(jnp.bfloat16)
    return hi, (a - hi.astype(jnp.float32)).astype(jnp.bfloat16)


def mask_kernel(gs, cs, geom, own, soft, feat, w_h, mw, fg, rt, feat_out, A, T, D, tgt, lg, w, V, P, sem):
    f32, bf16 = jnp.float32, jnp.bfloat16
    cnt = cs[0, 0]
    loads = [pltpu.make_async_copy(w_h.at[n], w.at[n], sem.at[n]) for n in range(4)]
    for load in loads:
        load.start()
    store = pltpu.make_async_copy(feat, feat_out, sem.at[4])
    store.start()
    zrow = jnp.zeros((256, 256), bf16)
    A[0] = zrow
    A[15] = zrow
    for u in range(1, 15):
        A[u, 0:16, :] = zrow[0:16]
        A[u, 240:256, :] = zrow[0:16]
    g = geom[0, 0]
    valid = lax.broadcasted_iota(jnp.int32, (16, 1), 0) < cnt

    def column(n):
        same = lax.broadcasted_iota(jnp.int32, (16, 16), 0) == lax.broadcasted_iota(
            jnp.int32, (16, 16), 1
        )
        return jnp.sum(jnp.where(same, g[n : n + 1], 0), axis=1, keepdims=True)

    def rep(col):
        return jnp.concatenate([col] * CROP, axis=0)

    lefts, widths = rep(column(1)), rep(column(3))
    heights = rep(jnp.where(valid, column(2), 0))
    row = lax.broadcasted_iota(jnp.int32, (ROWS, 1), 0)
    vv, kk = row // 16, row % 16
    in_w = vv < widths
    target = jnp.where(in_w, kk * 32 + lefts + vv, -1)
    lane = lax.broadcasted_iota(jnp.int32, (ROWS, 512), 1)
    pick = jnp.where(lane == target, 1.0, 0.0).astype(bf16)

    soft_rows = soft[0, 0]
    cell = lax.broadcasted_iota(jnp.int32, (CROP * CROP, 128), 0)
    step = lax.broadcasted_iota(jnp.int32, (CROP * CROP, 128), 1)
    for v in range(CROP):
        spread = jnp.where(cell == step * CROP + v, 1.0, 0.0).astype(bf16)
        tgt[v * 16 : (v + 1) * 16] = jnp.dot(soft_rows, spread, preferred_element_type=f32)

    def gather(u, c):
        strips = jnp.concatenate([feat[gs[0, 0, 0, k] + u] for k in range(16)], axis=0)
        crop = jnp.dot(pick, strips, preferred_element_type=f32)
        crop = jnp.where(u < heights, crop, 0.0)
        A[u + 1, 16:240, :] = crop.astype(bf16)
        return c

    lax.fori_loop(0, CROP, gather, 0)
    lg[...] = jnp.zeros_like(lg)

    def form(j):
        for m in range(7):
            d = [A[2 * m + i] for i in range(4)]
            T[j, m] = (d[0] - d[2], d[1] + d[2], d[2] - d[1], d[1] - d[3])[j]

    def taps(l):
        for n in range(0, 768, 256):
            a = w[l, n : n + 256].astype(f32) + w[l, 1536 + n : 1792 + n].astype(f32)
            b = w[l, 768 + n : 1024 + n].astype(f32)
            V[l, 0, n : n + 256] = (0.5 * (a + b)).astype(bf16)
            V[l, 1, n : n + 256] = (0.5 * (a - b)).astype(bf16)

    def kernel_of(l, j):
        return (w.at[l, 0:768], V.at[l, 0], V.at[l, 1], w.at[l, 1536:2304])[j]

    def shifted(j, t):
        return jnp.concatenate([T[j, m, t * 16 : t * 16 + ROWS, :] for m in range(7)], axis=0)

    def fwd_product(l, j):
        lhs = jnp.concatenate([shifted(j, t) for t in range(3)], axis=1)
        return jnp.dot(lhs, kernel_of(l, j)[...], preferred_element_type=f32)

    def bwd_product(l, j):
        ref = kernel_of(l, 3 - j if j in (0, 3) else j)
        acc = None
        for t in range(3):
            d = lax.dot_general(
                shifted(j, 2 - t), ref[t * 256 : (t + 1) * 256], (((1,), (1,)), ((), ())),
                preferred_element_type=f32,
            )
            acc = d if acc is None else acc + d
        return acc

    def finish_fwd(l, u, pre):
        act, slope = gelu_pair(pre)
        A[u + 1, 16:240, :] = act.astype(bf16)
        D[l, u] = slope.astype(bf16)

    def finish_last(l, u, pre):
        act, slope = gelu_pair(pre)
        m = mw[...].astype(f32).reshape(1, 256)
        logit = jnp.sum(act.astype(bf16).astype(f32) * m, axis=1, keepdims=True)
        sel = lax.broadcasted_iota(jnp.int32, (ROWS, 128), 1) == u
        lg[...] = jnp.where(sel, logit, lg[...])
        tg = tgt[:, u : u + 1]
        gl = jnp.where(in_w & (u < heights), 128.0 * (jax.nn.sigmoid(logit) - tg), 0.0)
        A[u + 1, 16:240, :] = (gl * m * slope).astype(bf16)

    def layer(l, product, finish, first, waiting, parity):
        lead = 3 if first == 0 else 0
        rest = 3 - lead
        p1, p2, p_lead, p_rest = P.at[0], P.at[1], P.at[2 + parity], P.at[4 + parity]
        form(lead)
        p_lead[...] = product(l, lead)
        waiting()
        for j in (1, 2, rest):
            form(j)
        p1[...] = product(l, 1)
        p2[...] = product(l, 2)
        p_rest[...] = product(l, rest)

        def done(odd, edge):
            for m in range(7):
                sl = slice(m * ROWS, (m + 1) * ROWS)
                x = p1[sl] - p2[sl] - edge[sl] if odd else p1[sl] + p2[sl] + edge[sl]
                finish(l, 2 * m + odd, x)

        other = 1 - first
        done(other, p_lead)
        return other, lambda: done(first, p_rest), 1 - parity

    loads[0].wait()
    taps(0)
    state = (0, lambda: None, 0)
    for l in range(4):
        state = layer(l, fwd_product, finish_last if l == 3 else finish_fwd, *state)
        if l < 3:
            loads[l + 1].wait()
            taps(l + 1)
    fg[...] = jnp.zeros_like(fg)
    state[1]()

    def products(l):
        for j in range(4):
            form(j)
        for j in range(4):
            P[j] = bwd_product(l, j)

    def rows_of(m, odd):
        sl = slice(m * ROWS, (m + 1) * ROWS)
        return P[1, sl] - P[2, sl] - P[3, sl] if odd else P[0, sl] + P[1, sl] + P[2, sl]

    def back(i, c):
        l = 3 - i
        products(l)
        for u in range(CROP):
            A[u + 1, 16:240, :] = (rows_of(u // 2, u % 2) * D[l - 1, u].astype(f32)).astype(bf16)
        return c

    lax.fori_loop(0, 3, back, 0)
    products(0)
    for u in range(CROP):
        grad = jnp.where(u < heights, rows_of(u // 2, u % 2), 0.0).astype(bf16)
        z = lax.dot_general(pick, grad, (((0,), (0,)), ((), ())), preferred_element_type=f32)
        for k in range(16):
            fg[gs[0, 0, 0, k] + u] += z[k * 32 : (k + 1) * 32]

    spot = lax.broadcasted_iota(jnp.int32, (128, 256), 1)
    from_u = lax.broadcasted_iota(jnp.int32, (128, 256), 0)
    flat = jnp.zeros((16, 256), f32)
    for v in range(CROP):
        spread = jnp.where((spot == from_u * CROP + v) & (from_u < CROP), 1.0, 0.0).astype(bf16)
        for part in halves(lg[v * 16 : (v + 1) * 16]):
            flat = flat + jnp.dot(part, spread, preferred_element_type=f32)
    flat = jnp.where(lax.broadcasted_iota(jnp.int32, (16, 256), 1) < CROP * CROP, flat, 1.0)
    used = lax.broadcasted_iota(jnp.int32, (16, 16), 1) < cnt
    sent = (own[0] == lax.broadcasted_iota(jnp.int32, (16, 16), 0)) & used
    sent = jnp.where(sent, 1.0, 0.0).astype(bf16)
    routed = jnp.zeros((16, 256), f32)
    for part in halves(flat):
        routed = routed + jnp.dot(sent, part, preferred_element_type=f32)
    for o in range(16):
        rt[o] = routed[o : o + 1]
    store.wait()


def mask_head(geometry, count, owner, soft, feat, conv_w, mask_w):
    V = pl.BlockSpec(memory_space=pltpu.VMEM)
    S = pl.BlockSpec(memory_space=pltpu.SMEM)
    H = pl.BlockSpec(memory_space=pl.ANY)
    return pl.pallas_call(
        mask_kernel,
        out_shape=(
            jax.ShapeDtypeStruct((32, 32, 256), jnp.float32),
            jax.ShapeDtypeStruct((16, 1, 256), jnp.float32),
            jax.ShapeDtypeStruct((32, 32, 256), jnp.bfloat16),
        ),
        in_specs=[S, S, V, V, V, V, H, V],
        out_specs=(V, V, H),
        scratch_shapes=[
            pltpu.VMEM((16, 256, 256), jnp.bfloat16),
            pltpu.VMEM((4, 7, 256, 256), jnp.bfloat16),
            pltpu.VMEM((3, 14, ROWS, 256), jnp.bfloat16),
            pltpu.VMEM((ROWS, 128), jnp.float32),
            pltpu.VMEM((ROWS, 128), jnp.float32),
            pltpu.VMEM((4, 2304, 256), jnp.bfloat16),
            pltpu.VMEM((4, 2, 768, 256), jnp.bfloat16),
            pltpu.VMEM((6, 7 * ROWS, 256), jnp.float32),
            pltpu.SemaphoreType.DMA((5,)),
        ],
        compiler_params=pltpu.CompilerParams(vmem_limit_bytes=63 << 20),
    )(geometry, count, geometry, owner, soft, feat, conv_w, mask_w)


def deal_kernel(outgoing, out, recv, send_sem, recv_sem):
    me, n = lax.axis_index("row"), lax.axis_size("row")
    col = lax.axis_index("col")
    barrier = pltpu.get_barrier_semaphore()
    for d in range(1, 16):
        pl.semaphore_signal(
            barrier, inc=1, device_id=(lax.rem(me + d, n), col), device_id_type=MESH
        )
    pl.semaphore_wait(barrier, 15)

    def copy_to(d, slot):
        peer = lax.rem(me + d, n)
        return pltpu.make_async_remote_copy(
            src_ref=outgoing.at[peer], dst_ref=recv.at[slot],
            send_sem=send_sem.at[d], recv_sem=recv_sem.at[d],
            device_id=(peer, col), device_id_type=MESH,
        )

    for d in range(1, 16):
        copy_to(d, me).start()
    recv[me] = outgoing[me]
    for d in range(1, 16):
        copy_to(d, lax.rem(me + n - d, n)).wait()
    got = jnp.concatenate([recv[i] for i in range(16)], axis=0)
    flag = jnp.where(got[:, 255:256] > 0.5, 1.0, 0.0)
    later = lax.broadcasted_iota(jnp.int32, (16, 16), 0) > lax.broadcasted_iota(
        jnp.int32, (16, 16), 1
    )
    place = jnp.dot(
        jnp.where(later, 1.0, 0.0).astype(jnp.bfloat16),
        jnp.broadcast_to(flag, (16, 128)).astype(jnp.bfloat16),
        preferred_element_type=jnp.float32,
    )[:, 0:1]
    rows = [
        jnp.sum(jnp.where((place == float(i)) & (flag > 0.5), got, 0.0), axis=0, keepdims=True)
        for i in range(BOX_OWN)
    ]
    out[0, 0] = jnp.concatenate(rows, axis=0)[:, 0 : CROP * CROP]


def deal_logits(outgoing):
    V = pl.BlockSpec(memory_space=pltpu.VMEM)
    return pl.pallas_call(
        deal_kernel,
        out_shape=jax.ShapeDtypeStruct((1, 1, BOX_OWN, CROP * CROP), jnp.float32),
        in_specs=[V],
        out_specs=V,
        scratch_shapes=[
            pltpu.VMEM((16, 1, 256), jnp.float32),
            pltpu.SemaphoreType.DMA((16,)),
            pltpu.SemaphoreType.DMA((16,)),
        ],
        compiler_params=pltpu.CompilerParams(collective_id=1, has_side_effects=True),
    )(outgoing)


def shards(
    tokens,
    first_gain,
    second_gain,
    joint_weight,
    merge_weight,
    expand_weight,
    shrink_weight,
    relative_bias,
    lateral_weight,
    conv_weight,
    mask_weight,
    box_geometry,
    box_counts,
    box_owner,
    soft_target,
):
    features = swin(
        tokens, first_gain, second_gain, joint_weight, merge_weight,
        expand_weight, shrink_weight, relative_bias, lateral_weight,
    )
    feature_grad, outgoing, features = mask_head(
        box_geometry.transpose(0, 1, 3, 2), box_counts, box_owner, soft_target, features,
        conv_weight, mask_weight,
    )
    return (features, feature_grad, deal_logits(outgoing))


def solution(mesh):
    placed = (
        P("row", "col", None),
        P(),
        P(),
        P(),
        P(),
        P(),
        P(),
        P(),
        P(),
        P(),
        P(),
        P("row", "col", None, None),
        P("row", "col"),
        P("row", "col", None),
        P("row", "col", None, None),
    )
    return jax.shard_map(
        shards,
        mesh=mesh,
        in_specs=placed,
        out_specs=(P("row", "col", None), P("row", "col", None), P("row", "col", None, None)),
        check_vma=False,
    )
```

```python
import functools
import jax
import jax.numpy as jnp
from jax import lax
from jax.experimental import pallas as pl
from jax.experimental.pallas import tpu as pltpu
from jax.sharding import PartitionSpec as P

CROP = 14
BOX_OWN = 8
EPSILON = 1e-05
G1 = 0.7978845608028654
G2 = G1 * 0.044715
ROWS = 224
MESH = pl.DeviceIdType.MESH


def norm_rows(x, gain):
    x = x - jnp.mean(x, axis=-1, keepdims=True)
    return x * lax.rsqrt(jnp.mean(x * x, axis=-1, keepdims=True) + EPSILON) * gain


def neighbours():
    row_at, row_n = lax.axis_index("row"), lax.axis_size("row")
    col_at, col_n = lax.axis_index("col"), lax.axis_size("col")
    found = []
    for dr in (-1, 0, 1):
        for dc in (-1, 0, 1):
            if dr == 0 and dc == 0:
                continue
            there = None
            for d, at, n in ((dr, row_at, row_n), (dc, col_at, col_n)):
                if d:
                    ok = at > 0 if d < 0 else at < n - 1
                    there = ok if there is None else there & ok
            found.append((dr, dc, there, (row_at + dr, col_at + dc)))
    return found


def swin_kernel(
    tok, g1, g2, wj_h, wm_h, we_h, ws_h, rb_h, wl_h, out,
    wj, wm, we, ws, rb, wl, E, J, ME, BB, ON,
    top, bottom, left, right, corner, send_sem, recv_sem, load_sem,
):
    f32, bf16 = jnp.float32, jnp.bfloat16
    row_at, row_n = lax.axis_index("row"), lax.axis_size("row")
    col_at, col_n = lax.axis_index("col"), lax.axis_size("col")
    loads = [
        pltpu.make_async_copy(src, dst, load_sem.at[n])
        for n, (src, dst) in enumerate(
            ((wj_h, wj), (rb_h, rb), (wm_h, wm), (we_h, we), (ws_h, ws), (wl_h, wl))
        )
    ]
    for load in loads:
        load.start()
    around = neighbours()
    barrier = pltpu.get_barrier_semaphore()
    for dr, dc, there, peer in around:

        @pl.when(there)
        def _(peer=peer):
            pl.semaphore_signal(barrier, inc=1, device_id=peer, device_id_type=MESH)

    near_rows = jnp.where(row_at > 0, 1, 0) + jnp.where(row_at < row_n - 1, 1, 0) + 1
    near_cols = jnp.where(col_at > 0, 1, 0) + jnp.where(col_at < col_n - 1, 1, 0) + 1
    pl.semaphore_wait(barrier, near_rows * near_cols - 1)

    def parts(dr, dc):
        if dc == 0:
            return (tok.at[0:4], bottom) if dr < 0 else (tok.at[28:32], top)
        span = slice(0, 8) if dc < 0 else slice(24, 32)
        if dr == 0:
            return tok.at[:, span], (right if dc < 0 else left)
        piece = tok.at[0:4, span] if dr < 0 else tok.at[28:32, span]
        return piece, corner.at[(0 if dr > 0 else 2) + (0 if dc > 0 else 1)]

    def copy_to(n, dr, dc, peer):
        src, dst = parts(dr, dc)
        return pltpu.make_async_remote_copy(
            src_ref=src, dst_ref=dst, send_sem=send_sem.at[n], recv_sem=recv_sem.at[n],
            device_id=peer, device_id_type=MESH,
        )

    for n, (dr, dc, there, peer) in enumerate(around):

        @pl.when(there)
        def _(n=n, dr=dr, dc=dc, peer=peer):
            copy_to(n, dr, dc, peer).start()

    def fill(r, carry):
        E[r + 4, 4:36, :] = tok[r].astype(f32)
        return carry

    lax.fori_loop(0, 32, fill, 0)
    loads[0].wait()
    loads[1].wait()
    for c in range(6):
        BB[c] = jnp.concatenate([rb[2 * c], rb[2 * c + 1]], axis=1)
    lane = lax.broadcasted_iota(jnp.int32, (64, 128), 1)
    head_of = lane // 32
    zero = jnp.zeros((64, 128), bf16)
    for h in range(4):
        ON[h * 64 : (h + 1) * 64] = jnp.where(head_of == h, 1.0, 0.0).astype(bf16)
    low = lane < 64
    qi = lax.broadcasted_iota(jnp.int32, (64, 128), 0)
    kj = lane % 64
    row_cut = (qi // 32) != (kj // 32)
    col_cut = ((qi // 4) % 2) != ((kj // 4) % 2)

    def windows(wi, across):
        first, last = across[0], across[-1]
        count = len(across)
        if count == last - first + 1:
            x = E[pl.ds(wi * 8, 8), first * 8 : (last + 1) * 8, :]
        else:
            x = jnp.concatenate([E[pl.ds(wi * 8, 8), j * 8 : (j + 1) * 8, :] for j in across], axis=1)
        x = norm_rows(x, g1[...].reshape(1, 1, 384))
        m = jnp.concatenate(
            [x[:, n * 8 : (n + 1) * 8, :].reshape(64, 384) for n in range(count)], axis=0
        ).astype(bf16)
        top_row = count * 64
        J[0:top_row, 0:384] = (
            jnp.dot(m, wj[:, 0:384], preferred_element_type=f32) * 32**-0.5
        ).astype(bf16)
        J[0:top_row, 384:1152] = jnp.dot(m, wj[:, 384:1152], preferred_element_type=f32).astype(bf16)
        row_flag = ((wi == 0) & (row_at == 0)) | ((wi == 4) & (row_at == row_n - 1))
        for n, j in enumerate(across):
            cut = row_cut & row_flag
            if j == 0:
                cut = cut | (col_cut & (col_at == 0))
            if j == 4:
                cut = cut | (col_cut & (col_at == col_n - 1))
            sl = slice(n * 64, (n + 1) * 64)
            for g in range(3):
                q = J[sl, g * 128 : (g + 1) * 128]
                k = J[sl, 384 + g * 128 : 384 + (g + 1) * 128]
                v = J[sl, 768 + g * 128 : 768 + (g + 1) * 128]
                kb = jnp.concatenate([jnp.where(head_of == h, k, zero) for h in range(4)], axis=0)
                s = lax.dot_general(q, kb, (((1,), (1,)), ((), ())), preferred_element_type=f32)
                es = []
                for c in range(2):
                    b = s[:, c * 128 : (c + 1) * 128] + BB[2 * g + c]
                    b = jnp.where(cut, -1e9, b)
                    m0 = jnp.max(jnp.where(low, b, -3e38), axis=1, keepdims=True)
                    m1 = jnp.max(jnp.where(low, -3e38, b), axis=1, keepdims=True)
                    es.append(jnp.exp(b - jnp.where(low, m0, m1)).astype(bf16))
                p = jnp.concatenate(es, axis=1)
                vb = jnp.concatenate([jnp.where(head_of == h, v, zero) for h in range(4)], axis=0)
                o = jnp.dot(p, jnp.concatenate([vb, ON[...]], axis=1), preferred_element_type=f32)
                o = o[:, 0:128] / o[:, 128:256]
                ME[pl.ds(wi * 8, 8), j * 8 : (j + 1) * 8, g * 128 : (g + 1) * 128] = o.reshape(8, 8, 128)

    def inner(n, carry):
        windows(n + 1, (1, 2, 3))
        return carry

    lax.fori_loop(0, 3, inner, 0)

    def land(dr, dc):
        rows = 0 if dr < 0 else 36
        if dc == 0:
            src = top if dr < 0 else bottom
            for r in range(4):
                yield (rows + r, slice(4, 36), lambda r=r: src[r].astype(f32))
            return
        span, part = (slice(0, 4), slice(4, 8)) if dc < 0 else (slice(36, 40), slice(0, 4))
        if dr == 0:
            src = left if dc < 0 else right
            for r in range(32):
                yield (4 + r, span, lambda r=r: src[r].astype(f32)[part])
            return
        piece = corner.at[(0 if dr < 0 else 2) + (0 if dc < 0 else 1)]
        for r in range(4):
            yield (rows + r, span, lambda r=r: piece[r].astype(f32)[part])

    for n, (dr, dc, there, peer) in enumerate(around):

        @pl.when(there)
        def _(n=n, dr=dr, dc=dc, peer=peer):
            copy_to(n, dr, dc, peer).wait_send()
            copy_to(len(around) - 1 - n, -dr, -dc, peer).wait_recv()
            for r, span, value in land(dr, dc):
                E[r, span, :] = value()

        @pl.when(jnp.logical_not(there))
        def _(dr=dr, dc=dc):
            for r, span, value in land(dr, dc):
                E[r, span, :] = jnp.zeros((span.stop - span.start, 384), f32)

    def sides(n, carry):
        windows(n + 1, (0, 4))
        return carry

    lax.fori_loop(0, 3, sides, 0)

    def ends(n, carry):
        windows(n * 4, (0, 1, 2, 3, 4))
        return carry

    lax.fori_loop(0, 2, ends, 0)
    for load in loads[2:]:
        load.wait()
    R = 16

    def tail(c, carry):
        r0 = c * R
        mixed = jnp.concatenate([ME[r0 + q + 4, 4:36, :] for q in range(R)], axis=0).astype(bf16)
        t = jnp.concatenate([tok[r0 + q] for q in range(R)], axis=0).astype(f32)
        res = t + jnp.dot(mixed, wm[...], preferred_element_type=f32)
        n2 = norm_rows(res, g2[...].reshape(1, 384)).astype(bf16)
        h = jnp.dot(n2, we[...], preferred_element_type=f32)
        h = (h * (0.5 + 0.5 * jnp.tanh(h * (G1 + G2 * (h * h))))).astype(bf16)
        b = (res + jnp.dot(h, ws[...], preferred_element_type=f32)).astype(bf16)
        f = jnp.dot(b, wl[...], preferred_element_type=f32).astype(bf16)
        for q in range(R):
            out[r0 + q] = f[q * 32 : (q + 1) * 32]
        return carry

    lax.fori_loop(0, 32 // R, tail, 0)


def swin(tok, g1, g2, wj, wm, we, ws, rb, wl):
    V = pl.BlockSpec(memory_space=pltpu.VMEM)
    A = pl.BlockSpec(memory_space=pl.ANY)
    weights = (wj, wm, we, ws, rb, wl)
    return pl.pallas_call(
        swin_kernel,
        out_shape=jax.ShapeDtypeStruct((32, 32, 256), jnp.bfloat16),
        in_specs=[V] * 3 + [A] * 6,
        out_specs=V,
        scratch_shapes=[pltpu.VMEM(w.shape, w.dtype) for w in weights]
        + [
            pltpu.VMEM((40, 40, 384), jnp.float32),
            pltpu.VMEM((320, 1152), jnp.bfloat16),
            pltpu.VMEM((40, 40, 384), jnp.float32),
            pltpu.VMEM((6, 64, 128), jnp.float32),
            pltpu.VMEM((256, 128), jnp.bfloat16),
            pltpu.VMEM((4, 32, 384), jnp.bfloat16),
            pltpu.VMEM((4, 32, 384), jnp.bfloat16),
            pltpu.VMEM((32, 8, 384), jnp.bfloat16),
            pltpu.VMEM((32, 8, 384), jnp.bfloat16),
            pltpu.VMEM((4, 4, 8, 384), jnp.bfloat16),
            pltpu.SemaphoreType.DMA((8,)),
            pltpu.SemaphoreType.DMA((8,)),
            pltpu.SemaphoreType.DMA((6,)),
        ],
        compiler_params=pltpu.CompilerParams(
            vmem_limit_bytes=63 << 20, collective_id=0, has_side_effects=True
        ),
    )(tok, g1, g2, wj, wm, we, ws, rb, wl)


def gelu_pair(x):
    x2 = x * x
    half = 0.5 + 0.5 * jnp.tanh(x * (G1 + G2 * x2))
    act = x * half
    slope = half + act * (1.0 - half) * (2.0 * G1 + (6.0 * G2) * x2)
    return act, slope


def halves(a):
    hi = a.astype(jnp.bfloat16)
    return hi, (a - hi.astype(jnp.float32)).astype(jnp.bfloat16)


def placement(g, cnt):
    valid = lax.broadcasted_iota(jnp.int32, (16, 1), 0) < cnt
    same = lax.broadcasted_iota(jnp.int32, (16, 16), 0) == lax.broadcasted_iota(
        jnp.int32, (16, 16), 1
    )

    def column(n):
        return jnp.sum(jnp.where(same, g[n : n + 1], 0), axis=1, keepdims=True)

    def rep(col):
        return jnp.concatenate([col] * CROP, axis=0)

    lefts, widths = rep(column(1)), rep(column(3))
    heights = rep(jnp.where(valid, column(2), 0))
    row = lax.broadcasted_iota(jnp.int32, (ROWS, 1), 0)
    vv, kk = row // 16, row % 16
    in_w = vv < widths
    target = jnp.where(in_w, kk * 32 + lefts + vv, -1)
    lane = lax.broadcasted_iota(jnp.int32, (ROWS, 512), 1)
    pick = jnp.where(lane == target, 1.0, 0.0).astype(jnp.bfloat16)
    return pick, in_w, heights


def mask_kernel(gs, cs, geom, own, soft, feat, w_h, mw, G, out, A, T, D, tgt, lg, w, V, P, rt, recv, sem, send_sem, recv_sem):
    f32, bf16 = jnp.float32, jnp.bfloat16
    cnt = cs[0, 0]
    loads = [pltpu.make_async_copy(w_h.at[n], w.at[n], sem.at[n]) for n in range(4)]
    for load in loads:
        load.start()
    me, n_row = lax.axis_index("row"), lax.axis_size("row")
    col_at = lax.axis_index("col")
    barrier = pltpu.get_barrier_semaphore()
    for d in range(1, 16):
        pl.semaphore_signal(
            barrier, inc=1, device_id=(lax.rem(me + d, n_row), col_at), device_id_type=MESH
        )

    def copy_to(d, slot):
        peer = lax.rem(me + d, n_row)
        return pltpu.make_async_remote_copy(
            src_ref=rt.at[peer], dst_ref=recv.at[slot],
            send_sem=send_sem.at[d], recv_sem=recv_sem.at[d],
            device_id=(peer, col_at), device_id_type=MESH,
        )

    zrow = jnp.zeros((256, 256), bf16)
    A[0] = zrow
    A[15] = zrow
    for u in range(1, 15):
        A[u, 0:16, :] = zrow[0:16]
        A[u, 240:256, :] = zrow[0:16]
    pick, in_w, heights = placement(geom[0, 0], cnt)
    soft_rows = soft[0, 0]
    cell = lax.broadcasted_iota(jnp.int32, (CROP * CROP, 128), 0)
    step = lax.broadcasted_iota(jnp.int32, (CROP * CROP, 128), 1)
    for v in range(CROP):
        spread = jnp.where(cell == step * CROP + v, 1.0, 0.0).astype(bf16)
        tgt[v * 16 : (v + 1) * 16] = jnp.dot(soft_rows, spread, preferred_element_type=f32)

    def gather(u, c):
        strips = jnp.concatenate([feat[gs[0, 0, 0, k] + u] for k in range(16)], axis=0)
        crop = jnp.dot(pick, strips, preferred_element_type=f32)
        crop = jnp.where(u < heights, crop, 0.0)
        A[u + 1, 16:240, :] = crop.astype(bf16)
        return c

    lax.fori_loop(0, CROP, gather, 0)
    lg[...] = jnp.zeros_like(lg)

    def form(j):
        for m in range(7):
            d = [A[2 * m + i] for i in range(4)]
            T[j, m] = (d[0] - d[2], d[1] + d[2], d[2] - d[1], d[1] - d[3])[j]

    def taps(l):
        for n in range(0, 768, 256):
            a = w[l, n : n + 256].astype(f32) + w[l, 1536 + n : 1792 + n].astype(f32)
            b = w[l, 768 + n : 1024 + n].astype(f32)
            V[l, 0, n : n + 256] = (0.5 * (a + b)).astype(bf16)
            V[l, 1, n : n + 256] = (0.5 * (a - b)).astype(bf16)

    def kernel_of(l, j):
        return (w.at[l, 0:768], V.at[l, 0], V.at[l, 1], w.at[l, 1536:2304])[j]

    def shifted(j, t):
        return jnp.concatenate([T[j, m, t * 16 : t * 16 + ROWS, :] for m in range(7)], axis=0)

    def fwd_product(l, j):
        lhs = jnp.concatenate([shifted(j, t) for t in range(3)], axis=1)
        return jnp.dot(lhs, kernel_of(l, j)[...], preferred_element_type=f32)

    def bwd_product(l, j):
        ref = kernel_of(l, 3 - j if j in (0, 3) else j)
        acc = None
        for t in range(3):
            d = lax.dot_general(
                shifted(j, 2 - t), ref[t * 256 : (t + 1) * 256], (((1,), (1,)), ((), ())),
                preferred_element_type=f32,
            )
            acc = d if acc is None else acc + d
        return acc

    def finish_fwd(l, u, pre):
        act, slope = gelu_pair(pre)
        A[u + 1, 16:240, :] = act.astype(bf16)
        D[l, u] = slope.astype(bf16)

    def finish_last(l, u, pre):
        act, slope = gelu_pair(pre)
        m = mw[...].astype(f32).reshape(1, 256)
        logit = jnp.sum(act.astype(bf16).astype(f32) * m, axis=1, keepdims=True)
        sel = lax.broadcasted_iota(jnp.int32, (ROWS, 128), 1) == u
        lg[...] = jnp.where(sel, logit, lg[...])
        tg = tgt[:, u : u + 1]
        gl = jnp.where(in_w & (u < heights), 128.0 * (jax.nn.sigmoid(logit) - tg), 0.0)
        A[u + 1, 16:240, :] = (gl * m * slope).astype(bf16)

    def layer(l, product, finish, first, waiting, parity):
        lead = 3 if first == 0 else 0
        rest = 3 - lead
        p1, p2, p_lead, p_rest = P.at[0], P.at[1], P.at[2 + parity], P.at[4 + parity]
        form(lead)
        p_lead[...] = product(l, lead)
        waiting()
        for j in (1, 2, rest):
            form(j)
        p1[...] = product(l, 1)
        p2[...] = product(l, 2)
        p_rest[...] = product(l, rest)

        def done(odd, edge):
            for m in range(7):
                sl = slice(m * ROWS, (m + 1) * ROWS)
                x = p1[sl] - p2[sl] - edge[sl] if odd else p1[sl] + p2[sl] + edge[sl]
                finish(l, 2 * m + odd, x)

        other = 1 - first
        done(other, p_lead)
        return other, lambda: done(first, p_rest), 1 - parity

    loads[0].wait()
    taps(0)
    state = (0, lambda: None, 0)
    for l in range(4):
        state = layer(l, fwd_product, finish_last if l == 3 else finish_fwd, *state)
        if l < 3:
            loads[l + 1].wait()
            taps(l + 1)
    state[1]()

    def products(l):
        for j in range(4):
            form(j)
        for j in range(4):
            P[j] = bwd_product(l, j)

    def rows_of(m, odd):
        sl = slice(m * ROWS, (m + 1) * ROWS)
        return P[1, sl] - P[2, sl] - P[3, sl] if odd else P[0, sl] + P[1, sl] + P[2, sl]

    spot = lax.broadcasted_iota(jnp.int32, (128, 256), 1)
    from_u = lax.broadcasted_iota(jnp.int32, (128, 256), 0)
    flat = jnp.zeros((16, 256), f32)
    for v in range(CROP):
        spread = jnp.where((spot == from_u * CROP + v) & (from_u < CROP), 1.0, 0.0).astype(bf16)
        for part in halves(lg[v * 16 : (v + 1) * 16]):
            flat = flat + jnp.dot(part, spread, preferred_element_type=f32)
    flat = jnp.where(lax.broadcasted_iota(jnp.int32, (16, 256), 1) < CROP * CROP, flat, 1.0)
    used = lax.broadcasted_iota(jnp.int32, (16, 16), 1) < cnt
    sent = (own[0] == lax.broadcasted_iota(jnp.int32, (16, 16), 0)) & used
    sent = jnp.where(sent, 1.0, 0.0).astype(bf16)
    routed = jnp.zeros((16, 256), f32)
    for part in halves(flat):
        routed = routed + jnp.dot(sent, part, preferred_element_type=f32)
    for o in range(16):
        rt[o] = routed[o : o + 1]
    recv[me] = rt[me]
    pl.semaphore_wait(barrier, 15)

    def back(i, c):
        l = 3 - i

        @pl.when(i == 1)
        def _():
            for d in range(1, 16):
                copy_to(d, me).start()

        products(l)
        for u in range(CROP):
            A[u + 1, 16:240, :] = (rows_of(u // 2, u % 2) * D[l - 1, u].astype(f32)).astype(bf16)
        return c

    lax.fori_loop(0, 3, back, 0)
    products(0)
    for u in range(CROP):
        G[u] = jnp.where(u < heights, rows_of(u // 2, u % 2), 0.0).astype(bf16)

    for d in range(1, 16):
        copy_to(d, lax.rem(me + n_row - d, n_row)).wait()
    got = jnp.concatenate([recv[i] for i in range(16)], axis=0)
    flag = jnp.where(got[:, 255:256] > 0.5, 1.0, 0.0)
    later = lax.broadcasted_iota(jnp.int32, (16, 16), 0) > lax.broadcasted_iota(
        jnp.int32, (16, 16), 1
    )
    place = jnp.dot(
        jnp.where(later, 1.0, 0.0).astype(bf16),
        jnp.broadcast_to(flag, (16, 128)).astype(bf16),
        preferred_element_type=f32,
    )[:, 0:1]
    rows = [
        jnp.sum(jnp.where((place == float(i)) & (flag > 0.5), got, 0.0), axis=0, keepdims=True)
        for i in range(BOX_OWN)
    ]
    out[0, 0] = jnp.concatenate(rows, axis=0)[:, 0 : CROP * CROP]


def place_kernel(gs, cs, geom, G, logits, feat, fg, logits_out, feat_out, sem):
    load = pltpu.make_async_copy(feat, feat_out, sem.at[0])
    load.start()
    pick, _, _ = placement(geom[0, 0], cs[0, 0])
    logits_out[...] = logits[...]
    fg[...] = jnp.zeros_like(fg)

    def put(u, c):
        z = lax.dot_general(pick, G[u], (((0,), (0,)), ((), ())), preferred_element_type=jnp.float32)
        for k in range(16):
            fg[gs[0, 0, 0, k] + u] += z[k * 32 : (k + 1) * 32]
        return c

    lax.fori_loop(0, CROP, put, 0)
    load.wait()


def mask_head(geometry, count, owner, soft, feat, conv_w, mask_w):
    V = pl.BlockSpec(memory_space=pltpu.VMEM)
    S = pl.BlockSpec(memory_space=pltpu.SMEM)
    H = pl.BlockSpec(memory_space=pl.ANY)
    grads, logits = pl.pallas_call(
        mask_kernel,
        out_shape=(
            jax.ShapeDtypeStruct((CROP, ROWS, 256), jnp.bfloat16),
            jax.ShapeDtypeStruct((1, 1, BOX_OWN, CROP * CROP), jnp.float32),
        ),
        in_specs=[S, S, V, V, V, V, H, V],
        out_specs=(V, V),
        scratch_shapes=[
            pltpu.VMEM((16, 256, 256), jnp.bfloat16),
            pltpu.VMEM((4, 7, 256, 256), jnp.bfloat16),
            pltpu.VMEM((3, 14, ROWS, 256), jnp.bfloat16),
            pltpu.VMEM((ROWS, 128), jnp.float32),
            pltpu.VMEM((ROWS, 128), jnp.float32),
            pltpu.VMEM((4, 2304, 256), jnp.bfloat16),
            pltpu.VMEM((4, 2, 768, 256), jnp.bfloat16),
            pltpu.VMEM((6, 7 * ROWS, 256), jnp.float32),
            pltpu.VMEM((16, 1, 256), jnp.float32),
            pltpu.VMEM((16, 1, 256), jnp.float32),
            pltpu.SemaphoreType.DMA((4,)),
            pltpu.SemaphoreType.DMA((16,)),
            pltpu.SemaphoreType.DMA((16,)),
        ],
        compiler_params=pltpu.CompilerParams(
            vmem_limit_bytes=63 << 20, collective_id=1, has_side_effects=True
        ),
    )(geometry, count, geometry, owner, soft, feat, conv_w, mask_w)
    return pl.pallas_call(
        place_kernel,
        out_shape=(
            jax.ShapeDtypeStruct((32, 32, 256), jnp.float32),
            jax.ShapeDtypeStruct((1, 1, BOX_OWN, CROP * CROP), jnp.float32),
            jax.ShapeDtypeStruct((32, 32, 256), jnp.bfloat16),
        ),
        in_specs=[S, S, V, V, V, V],
        out_specs=(V, V, H),
        scratch_shapes=[pltpu.SemaphoreType.DMA((1,))],
        compiler_params=pltpu.CompilerParams(vmem_limit_bytes=63 << 20),
    )(geometry, count, geometry, grads, logits, feat)


def shards(
    tokens,
    first_gain,
    second_gain,
    joint_weight,
    merge_weight,
    expand_weight,
    shrink_weight,
    relative_bias,
    lateral_weight,
    conv_weight,
    mask_weight,
    box_geometry,
    box_counts,
    box_owner,
    soft_target,
):
    features = swin(
        tokens, first_gain, second_gain, joint_weight, merge_weight,
        expand_weight, shrink_weight, relative_bias, lateral_weight,
    )
    feature_grad, logits, features = mask_head(
        box_geometry.transpose(0, 1, 3, 2), box_counts, box_owner, soft_target, features,
        conv_weight, mask_weight,
    )
    return (features, feature_grad, logits)


def solution(mesh):
    placed = (
        P("row", "col", None),
        P(),
        P(),
        P(),
        P(),
        P(),
        P(),
        P(),
        P(),
        P(),
        P(),
        P("row", "col", None, None),
        P("row", "col"),
        P("row", "col", None),
        P("row", "col", None, None),
    )
    return jax.shard_map(
        shards,
        mesh=mesh,
        in_specs=placed,
        out_specs=(P("row", "col", None), P("row", "col", None), P("row", "col", None, None)),
        check_vma=False,
    )
```

```python
import functools
import jax
import jax.numpy as jnp
from jax import lax
from jax.experimental import pallas as pl
from jax.experimental.pallas import tpu as pltpu
from jax.sharding import PartitionSpec as P

CROP = 14
BOX_OWN = 8
EPSILON = 1e-05
G1 = 0.7978845608028654
G2 = G1 * 0.044715
ROWS = 224
MESH = pl.DeviceIdType.MESH


def norm_rows(x, gain):
    x = x - jnp.mean(x, axis=-1, keepdims=True)
    return x * lax.rsqrt(jnp.mean(x * x, axis=-1, keepdims=True) + EPSILON) * gain


def neighbours():
    row_at, row_n = lax.axis_index("row"), lax.axis_size("row")
    col_at, col_n = lax.axis_index("col"), lax.axis_size("col")
    found = []
    for dr in (-1, 0, 1):
        for dc in (-1, 0, 1):
            if dr == 0 and dc == 0:
                continue
            there = None
            for d, at, n in ((dr, row_at, row_n), (dc, col_at, col_n)):
                if d:
                    ok = at > 0 if d < 0 else at < n - 1
                    there = ok if there is None else there & ok
            found.append((dr, dc, there, (row_at + dr, col_at + dc)))
    return found


def swin_kernel(
    tok, g1, g2, wj_h, wm_h, we_h, ws_h, rb_h, wl_h, out,
    wj, wm, we, ws, rb, wl, E, J, ME, BB, ON,
    top, bottom, left, right, corner, send_sem, recv_sem, load_sem,
):
    f32, bf16 = jnp.float32, jnp.bfloat16
    row_at, row_n = lax.axis_index("row"), lax.axis_size("row")
    col_at, col_n = lax.axis_index("col"), lax.axis_size("col")
    loads = [
        pltpu.make_async_copy(src, dst, load_sem.at[n])
        for n, (src, dst) in enumerate(
            ((wj_h, wj), (rb_h, rb), (wm_h, wm), (we_h, we), (ws_h, ws), (wl_h, wl))
        )
    ]
    for load in loads:
        load.start()
    around = neighbours()
    barrier = pltpu.get_barrier_semaphore()
    for dr, dc, there, peer in around:

        @pl.when(there)
        def _(peer=peer):
            pl.semaphore_signal(barrier, inc=1, device_id=peer, device_id_type=MESH)

    near_rows = jnp.where(row_at > 0, 1, 0) + jnp.where(row_at < row_n - 1, 1, 0) + 1
    near_cols = jnp.where(col_at > 0, 1, 0) + jnp.where(col_at < col_n - 1, 1, 0) + 1
    pl.semaphore_wait(barrier, near_rows * near_cols - 1)

    def parts(dr, dc):
        if dc == 0:
            return (tok.at[0:4], bottom) if dr < 0 else (tok.at[28:32], top)
        span = slice(0, 8) if dc < 0 else slice(24, 32)
        if dr == 0:
            return tok.at[:, span], (right if dc < 0 else left)
        piece = tok.at[0:4, span] if dr < 0 else tok.at[28:32, span]
        return piece, corner.at[(0 if dr > 0 else 2) + (0 if dc > 0 else 1)]

    def copy_to(n, dr, dc, peer):
        src, dst = parts(dr, dc)
        return pltpu.make_async_remote_copy(
            src_ref=src, dst_ref=dst, send_sem=send_sem.at[n], recv_sem=recv_sem.at[n],
            device_id=peer, device_id_type=MESH,
        )

    for n, (dr, dc, there, peer) in enumerate(around):

        @pl.when(there)
        def _(n=n, dr=dr, dc=dc, peer=peer):
            copy_to(n, dr, dc, peer).start()

    def fill(r, carry):
        E[r + 4, 4:36, :] = tok[r].astype(f32)
        return carry

    lax.fori_loop(0, 32, fill, 0)
    loads[0].wait()
    loads[1].wait()
    for c in range(6):
        BB[c] = jnp.concatenate([rb[2 * c], rb[2 * c + 1]], axis=1)
    lane = lax.broadcasted_iota(jnp.int32, (64, 128), 1)
    head_of = lane // 32
    zero = jnp.zeros((64, 128), bf16)
    for h in range(4):
        ON[h * 64 : (h + 1) * 64] = jnp.where(head_of == h, 1.0, 0.0).astype(bf16)
    low = lane < 64
    qi = lax.broadcasted_iota(jnp.int32, (64, 128), 0)
    kj = lane % 64
    row_cut = (qi // 32) != (kj // 32)
    col_cut = ((qi // 4) % 2) != ((kj // 4) % 2)

    def windows(wi, across):
        first, last = across[0], across[-1]
        count = len(across)
        if count == last - first + 1:
            x = E[pl.ds(wi * 8, 8), first * 8 : (last + 1) * 8, :]
        else:
            x = jnp.concatenate([E[pl.ds(wi * 8, 8), j * 8 : (j + 1) * 8, :] for j in across], axis=1)
        x = norm_rows(x, g1[...].reshape(1, 1, 384))
        m = jnp.concatenate(
            [x[:, n * 8 : (n + 1) * 8, :].reshape(64, 384) for n in range(count)], axis=0
        ).astype(bf16)
        top_row = count * 64
        J[0:top_row, 0:384] = (
            jnp.dot(m, wj[:, 0:384], preferred_element_type=f32) * 32**-0.5
        ).astype(bf16)
        J[0:top_row, 384:1152] = jnp.dot(m, wj[:, 384:1152], preferred_element_type=f32).astype(bf16)
        row_flag = ((wi == 0) & (row_at == 0)) | ((wi == 4) & (row_at == row_n - 1))
        for n, j in enumerate(across):
            cut = row_cut & row_flag
            if j == 0:
                cut = cut | (col_cut & (col_at == 0))
            if j == 4:
                cut = cut | (col_cut & (col_at == col_n - 1))
            sl = slice(n * 64, (n + 1) * 64)
            for g in range(3):
                q = J[sl, g * 128 : (g + 1) * 128]
                k = J[sl, 384 + g * 128 : 384 + (g + 1) * 128]
                v = J[sl, 768 + g * 128 : 768 + (g + 1) * 128]
                kb = jnp.concatenate([jnp.where(head_of == h, k, zero) for h in range(4)], axis=0)
                s = lax.dot_general(q, kb, (((1,), (1,)), ((), ())), preferred_element_type=f32)
                es = []
                for c in range(2):
                    b = s[:, c * 128 : (c + 1) * 128] + BB[2 * g + c]
                    b = jnp.where(cut, -1e9, b)
                    m0 = jnp.max(jnp.where(low, b, -3e38), axis=1, keepdims=True)
                    m1 = jnp.max(jnp.where(low, -3e38, b), axis=1, keepdims=True)
                    es.append(jnp.exp(b - jnp.where(low, m0, m1)).astype(bf16))
                p = jnp.concatenate(es, axis=1)
                vb = jnp.concatenate([jnp.where(head_of == h, v, zero) for h in range(4)], axis=0)
                o = jnp.dot(p, jnp.concatenate([vb, ON[...]], axis=1), preferred_element_type=f32)
                o = o[:, 0:128] / o[:, 128:256]
                ME[pl.ds(wi * 8, 8), j * 8 : (j + 1) * 8, g * 128 : (g + 1) * 128] = o.reshape(8, 8, 128)

    def inner(n, carry):
        windows(n + 1, (1, 2, 3))
        return carry

    lax.fori_loop(0, 3, inner, 0)

    def land(dr, dc):
        rows = 0 if dr < 0 else 36
        if dc == 0:
            src = top if dr < 0 else bottom
            for r in range(4):
                yield (rows + r, slice(4, 36), lambda r=r: src[r].astype(f32))
            return
        span, part = (slice(0, 4), slice(4, 8)) if dc < 0 else (slice(36, 40), slice(0, 4))
        if dr == 0:
            src = left if dc < 0 else right
            for r in range(32):
                yield (4 + r, span, lambda r=r: src[r].astype(f32)[part])
            return
        piece = corner.at[(0 if dr < 0 else 2) + (0 if dc < 0 else 1)]
        for r in range(4):
            yield (rows + r, span, lambda r=r: piece[r].astype(f32)[part])

    for n, (dr, dc, there, peer) in enumerate(around):

        @pl.when(there)
        def _(n=n, dr=dr, dc=dc, peer=peer):
            copy_to(n, dr, dc, peer).wait_send()
            copy_to(len(around) - 1 - n, -dr, -dc, peer).wait_recv()
            for r, span, value in land(dr, dc):
                E[r, span, :] = value()

        @pl.when(jnp.logical_not(there))
        def _(dr=dr, dc=dc):
            for r, span, value in land(dr, dc):
                E[r, span, :] = jnp.zeros((span.stop - span.start, 384), f32)

    def sides(n, carry):
        windows(n + 1, (0, 4))
        return carry

    lax.fori_loop(0, 3, sides, 0)

    def ends(n, carry):
        windows(n * 4, (0, 1, 2, 3, 4))
        return carry

    lax.fori_loop(0, 2, ends, 0)
    for load in loads[2:]:
        load.wait()
    R = 32

    def tail(c, carry):
        r0 = c * R
        mixed = jnp.concatenate([ME[r0 + q + 4, 4:36, :] for q in range(R)], axis=0).astype(bf16)
        t = jnp.concatenate([tok[r0 + q] for q in range(R)], axis=0).astype(f32)
        res = t + jnp.dot(mixed, wm[...], preferred_element_type=f32)
        n2 = norm_rows(res, g2[...].reshape(1, 384)).astype(bf16)
        h = jnp.dot(n2, we[...], preferred_element_type=f32)
        h = (h * (0.5 + 0.5 * jnp.tanh(h * (G1 + G2 * (h * h))))).astype(bf16)
        b = (res + jnp.dot(h, ws[...], preferred_element_type=f32)).astype(bf16)
        f = jnp.dot(b, wl[...], preferred_element_type=f32).astype(bf16)
        for q in range(R):
            out[r0 + q] = f[q * 32 : (q + 1) * 32]
        return carry

    lax.fori_loop(0, 32 // R, tail, 0)


def swin(tok, g1, g2, wj, wm, we, ws, rb, wl):
    V = pl.BlockSpec(memory_space=pltpu.VMEM)
    A = pl.BlockSpec(memory_space=pl.ANY)
    weights = (wj, wm, we, ws, rb, wl)
    return pl.pallas_call(
        swin_kernel,
        out_shape=jax.ShapeDtypeStruct((32, 32, 256), jnp.bfloat16),
        in_specs=[V] * 3 + [A] * 6,
        out_specs=V,
        scratch_shapes=[pltpu.VMEM(w.shape, w.dtype) for w in weights]
        + [
            pltpu.VMEM((40, 40, 384), jnp.float32),
            pltpu.VMEM((320, 1152), jnp.bfloat16),
            pltpu.VMEM((40, 40, 384), jnp.float32),
            pltpu.VMEM((6, 64, 128), jnp.float32),
            pltpu.VMEM((256, 128), jnp.bfloat16),
            pltpu.VMEM((4, 32, 384), jnp.bfloat16),
            pltpu.VMEM((4, 32, 384), jnp.bfloat16),
            pltpu.VMEM((32, 8, 384), jnp.bfloat16),
            pltpu.VMEM((32, 8, 384), jnp.bfloat16),
            pltpu.VMEM((4, 4, 8, 384), jnp.bfloat16),
            pltpu.SemaphoreType.DMA((8,)),
            pltpu.SemaphoreType.DMA((8,)),
            pltpu.SemaphoreType.DMA((6,)),
        ],
        compiler_params=pltpu.CompilerParams(
            vmem_limit_bytes=63 << 20, collective_id=0, has_side_effects=True
        ),
    )(tok, g1, g2, wj, wm, we, ws, rb, wl)


def gelu_pair(x):
    x2 = x * x
    half = 0.5 + 0.5 * jnp.tanh(x * (G1 + G2 * x2))
    act = x * half
    slope = half + act * (1.0 - half) * (2.0 * G1 + (6.0 * G2) * x2)
    return act, slope


def halves(a):
    hi = a.astype(jnp.bfloat16)
    return hi, (a - hi.astype(jnp.float32)).astype(jnp.bfloat16)


def placement(g, cnt):
    valid = lax.broadcasted_iota(jnp.int32, (16, 1), 0) < cnt
    same = lax.broadcasted_iota(jnp.int32, (16, 16), 0) == lax.broadcasted_iota(
        jnp.int32, (16, 16), 1
    )

    def column(n):
        return jnp.sum(jnp.where(same, g[n : n + 1], 0), axis=1, keepdims=True)

    def rep(col):
        return jnp.concatenate([col] * CROP, axis=0)

    lefts, widths = rep(column(1)), rep(column(3))
    heights = rep(jnp.where(valid, column(2), 0))
    row = lax.broadcasted_iota(jnp.int32, (ROWS, 1), 0)
    vv, kk = row // 16, row % 16
    in_w = vv < widths
    target = jnp.where(in_w, kk * 32 + lefts + vv, -1)
    lane = lax.broadcasted_iota(jnp.int32, (ROWS, 512), 1)
    pick = jnp.where(lane == target, 1.0, 0.0).astype(jnp.bfloat16)
    return pick, in_w, heights


def mask_kernel(gs, cs, geom, own, soft, feat, w_h, mw, G, out, A, T, D, tgt, lg, w, V, P, rt, recv, sem, send_sem, recv_sem):
    f32, bf16 = jnp.float32, jnp.bfloat16
    cnt = cs[0, 0]
    loads = [pltpu.make_async_copy(w_h.at[n], w.at[n], sem.at[n]) for n in range(4)]
    for load in loads:
        load.start()
    me, n_row = lax.axis_index("row"), lax.axis_size("row")
    col_at = lax.axis_index("col")
    barrier = pltpu.get_barrier_semaphore()
    for d in range(1, 16):
        pl.semaphore_signal(
            barrier, inc=1, device_id=(lax.rem(me + d, n_row), col_at), device_id_type=MESH
        )

    def copy_to(d, slot):
        peer = lax.rem(me + d, n_row)
        return pltpu.make_async_remote_copy(
            src_ref=rt.at[peer], dst_ref=recv.at[slot],
            send_sem=send_sem.at[d], recv_sem=recv_sem.at[d],
            device_id=(peer, col_at), device_id_type=MESH,
        )

    zrow = jnp.zeros((256, 256), bf16)
    A[0] = zrow
    A[15] = zrow
    for u in range(1, 15):
        A[u, 0:16, :] = zrow[0:16]
        A[u, 240:256, :] = zrow[0:16]
    pick, in_w, heights = placement(geom[0, 0], cnt)
    soft_rows = soft[0, 0]
    cell = lax.broadcasted_iota(jnp.int32, (CROP * CROP, 128), 0)
    step = lax.broadcasted_iota(jnp.int32, (CROP * CROP, 128), 1)
    for v in range(CROP):
        spread = jnp.where(cell == step * CROP + v, 1.0, 0.0).astype(bf16)
        tgt[v * 16 : (v + 1) * 16] = jnp.dot(soft_rows, spread, preferred_element_type=f32)

    def gather(u, c):
        strips = jnp.concatenate([feat[gs[0, 0, 0, k] + u] for k in range(16)], axis=0)
        crop = jnp.dot(pick, strips, preferred_element_type=f32)
        crop = jnp.where(u < heights, crop, 0.0)
        A[u + 1, 16:240, :] = crop.astype(bf16)
        return c

    lax.fori_loop(0, CROP, gather, 0)
    lg[...] = jnp.zeros_like(lg)

    def form(j):
        for m in range(7):
            d = [A[2 * m + i] for i in range(4)]
            T[j, m] = (d[0] - d[2], d[1] + d[2], d[2] - d[1], d[1] - d[3])[j]

    def taps(l):
        for n in range(0, 768, 256):
            a = w[l, n : n + 256].astype(f32) + w[l, 1536 + n : 1792 + n].astype(f32)
            b = w[l, 768 + n : 1024 + n].astype(f32)
            V[l, 0, n : n + 256] = (0.5 * (a + b)).astype(bf16)
            V[l, 1, n : n + 256] = (0.5 * (a - b)).astype(bf16)

    def kernel_of(l, j):
        return (w.at[l, 0:768], V.at[l, 0], V.at[l, 1], w.at[l, 1536:2304])[j]

    def shifted(j, t):
        return jnp.concatenate([T[j, m, t * 16 : t * 16 + ROWS, :] for m in range(7)], axis=0)

    def fwd_product(l, j):
        lhs = jnp.concatenate([shifted(j, t) for t in range(3)], axis=1)
        return jnp.dot(lhs, kernel_of(l, j)[...], preferred_element_type=f32)

    def bwd_product(l, j):
        ref = kernel_of(l, 3 - j if j in (0, 3) else j)
        acc = None
        for t in range(3):
            d = lax.dot_general(
                shifted(j, 2 - t), ref[t * 256 : (t + 1) * 256], (((1,), (1,)), ((), ())),
                preferred_element_type=f32,
            )
            acc = d if acc is None else acc + d
        return acc

    def finish_fwd(l, u, pre):
        act, slope = gelu_pair(pre)
        A[u + 1, 16:240, :] = act.astype(bf16)
        D[l, u] = slope.astype(bf16)

    def finish_last(l, u, pre):
        act, slope = gelu_pair(pre)
        m = mw[...].astype(f32).reshape(1, 256)
        logit = jnp.sum(act.astype(bf16).astype(f32) * m, axis=1, keepdims=True)
        sel = lax.broadcasted_iota(jnp.int32, (ROWS, 128), 1) == u
        lg[...] = jnp.where(sel, logit, lg[...])
        tg = tgt[:, u : u + 1]
        gl = jnp.where(in_w & (u < heights), 128.0 * (jax.nn.sigmoid(logit) - tg), 0.0)
        A[u + 1, 16:240, :] = (gl * m * slope).astype(bf16)

    def layer(l, product, finish, first, waiting, parity):
        lead = 3 if first == 0 else 0
        rest = 3 - lead
        p1, p2, p_lead, p_rest = P.at[0], P.at[1], P.at[2 + parity], P.at[4 + parity]
        form(lead)
        p_lead[...] = product(l, lead)
        waiting()
        for j in (1, 2, rest):
            form(j)
        p1[...] = product(l, 1)
        p2[...] = product(l, 2)
        p_rest[...] = product(l, rest)

        def done(odd, edge):
            for m in range(7):
                sl = slice(m * ROWS, (m + 1) * ROWS)
                x = p1[sl] - p2[sl] - edge[sl] if odd else p1[sl] + p2[sl] + edge[sl]
                finish(l, 2 * m + odd, x)

        other = 1 - first
        done(other, p_lead)
        return other, lambda: done(first, p_rest), 1 - parity

    loads[0].wait()
    taps(0)
    state = (0, lambda: None, 0)
    for l in range(4):
        state = layer(l, fwd_product, finish_last if l == 3 else finish_fwd, *state)
        if l < 3:
            loads[l + 1].wait()
            taps(l + 1)
    state[1]()

    def products(l):
        for j in range(4):
            form(j)
        for j in range(4):
            P[j] = bwd_product(l, j)

    def rows_of(m, odd):
        sl = slice(m * ROWS, (m + 1) * ROWS)
        return P[1, sl] - P[2, sl] - P[3, sl] if odd else P[0, sl] + P[1, sl] + P[2, sl]

    spot = lax.broadcasted_iota(jnp.int32, (128, 256), 1)
    from_u = lax.broadcasted_iota(jnp.int32, (128, 256), 0)
    flat = jnp.zeros((16, 256), f32)
    for v in range(CROP):
        spread = jnp.where((spot == from_u * CROP + v) & (from_u < CROP), 1.0, 0.0).astype(bf16)
        for part in halves(lg[v * 16 : (v + 1) * 16]):
            flat = flat + jnp.dot(part, spread, preferred_element_type=f32)
    flat = jnp.where(lax.broadcasted_iota(jnp.int32, (16, 256), 1) < CROP * CROP, flat, 1.0)
    used = lax.broadcasted_iota(jnp.int32, (16, 16), 1) < cnt
    sent = (own[0] == lax.broadcasted_iota(jnp.int32, (16, 16), 0)) & used
    sent = jnp.where(sent, 1.0, 0.0).astype(bf16)
    routed = jnp.zeros((16, 256), f32)
    for part in halves(flat):
        routed = routed + jnp.dot(sent, part, preferred_element_type=f32)
    for o in range(16):
        rt[o] = routed[o : o + 1]
    recv[me] = rt[me]
    pl.semaphore_wait(barrier, 15)

    def back(i, c):
        l = 3 - i

        @pl.when(i == 1)
        def _():
            for d in range(1, 16):
                copy_to(d, me).start()

        products(l)
        for u in range(CROP):
            A[u + 1, 16:240, :] = (rows_of(u // 2, u % 2) * D[l - 1, u].astype(f32)).astype(bf16)
        return c

    lax.fori_loop(0, 3, back, 0)
    products(0)
    for u in range(CROP):
        G[u] = jnp.where(u < heights, rows_of(u // 2, u % 2), 0.0).astype(bf16)

    for d in range(1, 16):
        copy_to(d, lax.rem(me + n_row - d, n_row)).wait()
    got = jnp.concatenate([recv[i] for i in range(16)], axis=0)
    flag = jnp.where(got[:, 255:256] > 0.5, 1.0, 0.0)
    later = lax.broadcasted_iota(jnp.int32, (16, 16), 0) > lax.broadcasted_iota(
        jnp.int32, (16, 16), 1
    )
    place = jnp.dot(
        jnp.where(later, 1.0, 0.0).astype(bf16),
        jnp.broadcast_to(flag, (16, 128)).astype(bf16),
        preferred_element_type=f32,
    )[:, 0:1]
    rows = [
        jnp.sum(jnp.where((place == float(i)) & (flag > 0.5), got, 0.0), axis=0, keepdims=True)
        for i in range(BOX_OWN)
    ]
    out[0, 0] = jnp.concatenate(rows, axis=0)[:, 0 : CROP * CROP]


def place_kernel(gs, cs, geom, G, logits, feat, fg, logits_out, feat_out, PT, sem):
    load = pltpu.make_async_copy(feat, feat_out, sem.at[0])
    load.start()
    pick, _, _ = placement(geom[0, 0], cs[0, 0])
    PT[...] = pick.astype(jnp.float32).T.astype(jnp.bfloat16)
    logits_out[...] = logits[...]
    fg[...] = jnp.zeros_like(fg)

    def put(i, c):
        for q in range(2):
            u = 2 * i + q
            z = jnp.dot(PT[...], G[u], preferred_element_type=jnp.float32)
            for k in range(16):
                fg[gs[0, 0, 0, k] + u] += z[k * 32 : (k + 1) * 32]
        return c

    lax.fori_loop(0, CROP // 2, put, 0)
    load.wait()


def mask_head(geometry, count, owner, soft, feat, conv_w, mask_w):
    V = pl.BlockSpec(memory_space=pltpu.VMEM)
    S = pl.BlockSpec(memory_space=pltpu.SMEM)
    H = pl.BlockSpec(memory_space=pl.ANY)
    grads, logits = pl.pallas_call(
        mask_kernel,
        out_shape=(
            jax.ShapeDtypeStruct((CROP, ROWS, 256), jnp.bfloat16),
            jax.ShapeDtypeStruct((1, 1, BOX_OWN, CROP * CROP), jnp.float32),
        ),
        in_specs=[S, S, V, V, V, V, H, V],
        out_specs=(V, V),
        scratch_shapes=[
            pltpu.VMEM((16, 256, 256), jnp.bfloat16),
            pltpu.VMEM((4, 7, 256, 256), jnp.bfloat16),
            pltpu.VMEM((3, 14, ROWS, 256), jnp.bfloat16),
            pltpu.VMEM((ROWS, 128), jnp.float32),
            pltpu.VMEM((ROWS, 128), jnp.float32),
            pltpu.VMEM((4, 2304, 256), jnp.bfloat16),
            pltpu.VMEM((4, 2, 768, 256), jnp.bfloat16),
            pltpu.VMEM((6, 7 * ROWS, 256), jnp.float32),
            pltpu.VMEM((16, 1, 256), jnp.float32),
            pltpu.VMEM((16, 1, 256), jnp.float32),
            pltpu.SemaphoreType.DMA((4,)),
            pltpu.SemaphoreType.DMA((16,)),
            pltpu.SemaphoreType.DMA((16,)),
        ],
        compiler_params=pltpu.CompilerParams(
            vmem_limit_bytes=63 << 20, collective_id=1, has_side_effects=True
        ),
    )(geometry, count, geometry, owner, soft, feat, conv_w, mask_w)
    return pl.pallas_call(
        place_kernel,
        out_shape=(
            jax.ShapeDtypeStruct((32, 32, 256), jnp.float32),
            jax.ShapeDtypeStruct((1, 1, BOX_OWN, CROP * CROP), jnp.float32),
            jax.ShapeDtypeStruct((32, 32, 256), jnp.bfloat16),
        ),
        in_specs=[S, S, V, V, V, V],
        out_specs=(V, V, H),
        scratch_shapes=[pltpu.VMEM((512, ROWS), jnp.bfloat16), pltpu.SemaphoreType.DMA((1,))],
        compiler_params=pltpu.CompilerParams(vmem_limit_bytes=63 << 20),
    )(geometry, count, geometry, grads, logits, feat)


def shards(
    tokens,
    first_gain,
    second_gain,
    joint_weight,
    merge_weight,
    expand_weight,
    shrink_weight,
    relative_bias,
    lateral_weight,
    conv_weight,
    mask_weight,
    box_geometry,
    box_counts,
    box_owner,
    soft_target,
):
    features = swin(
        tokens, first_gain, second_gain, joint_weight, merge_weight,
        expand_weight, shrink_weight, relative_bias, lateral_weight,
    )
    feature_grad, logits, features = mask_head(
        box_geometry.transpose(0, 1, 3, 2), box_counts, box_owner, soft_target, features,
        conv_weight, mask_weight,
    )
    return (features, feature_grad, logits)


def solution(mesh):
    placed = (
        P("row", "col", None),
        P(),
        P(),
        P(),
        P(),
        P(),
        P(),
        P(),
        P(),
        P(),
        P(),
        P("row", "col", None, None),
        P("row", "col"),
        P("row", "col", None),
        P("row", "col", None, None),
    )
    return jax.shard_map(
        shards,
        mesh=mesh,
        in_specs=placed,
        out_specs=(P("row", "col", None), P("row", "col", None), P("row", "col", None, None)),
        check_vma=False,
    )
```

```python
import functools
import jax
import jax.numpy as jnp
from jax import lax
from jax.experimental import pallas as pl
from jax.experimental.pallas import tpu as pltpu
from jax.sharding import PartitionSpec as P

CROP = 14
BOX_OWN = 8
EPSILON = 1e-05
G1 = 0.7978845608028654
G2 = G1 * 0.044715
ROWS = 224
MESH = pl.DeviceIdType.MESH


def norm_rows(x, gain):
    x = x - jnp.mean(x, axis=-1, keepdims=True)
    return x * lax.rsqrt(jnp.mean(x * x, axis=-1, keepdims=True) + EPSILON) * gain


def neighbours():
    row_at, row_n = lax.axis_index("row"), lax.axis_size("row")
    col_at, col_n = lax.axis_index("col"), lax.axis_size("col")
    found = []
    for dr in (-1, 0, 1):
        for dc in (-1, 0, 1):
            if dr == 0 and dc == 0:
                continue
            there = None
            for d, at, n in ((dr, row_at, row_n), (dc, col_at, col_n)):
                if d:
                    ok = at > 0 if d < 0 else at < n - 1
                    there = ok if there is None else there & ok
            found.append((dr, dc, there, (row_at + dr, col_at + dc)))
    return found


def swin_kernel(
    tok, g1, g2, wj_h, wm_h, we_h, ws_h, rb_h, wl_h, out,
    wj, wm, we, ws, rb, wl, E, J, ME, BB, ON,
    top, bottom, left, right, corner, send_sem, recv_sem, load_sem,
):
    f32, bf16 = jnp.float32, jnp.bfloat16
    row_at, row_n = lax.axis_index("row"), lax.axis_size("row")
    col_at, col_n = lax.axis_index("col"), lax.axis_size("col")
    loads = [
        pltpu.make_async_copy(src, dst, load_sem.at[n])
        for n, (src, dst) in enumerate(
            ((wj_h, wj), (rb_h, rb), (wm_h, wm), (we_h, we), (ws_h, ws), (wl_h, wl))
        )
    ]
    for load in loads:
        load.start()
    around = neighbours()
    barrier = pltpu.get_barrier_semaphore()
    for dr, dc, there, peer in around:

        @pl.when(there)
        def _(peer=peer):
            pl.semaphore_signal(barrier, inc=1, device_id=peer, device_id_type=MESH)

    def parts(dr, dc):
        if dc == 0:
            return (tok.at[0:4], bottom) if dr < 0 else (tok.at[28:32], top)
        span = slice(0, 8) if dc < 0 else slice(24, 32)
        if dr == 0:
            return tok.at[:, span], (right if dc < 0 else left)
        piece = tok.at[0:4, span] if dr < 0 else tok.at[28:32, span]
        return piece, corner.at[(0 if dr > 0 else 2) + (0 if dc > 0 else 1)]

    def copy_to(n, dr, dc, peer):
        src, dst = parts(dr, dc)
        return pltpu.make_async_remote_copy(
            src_ref=src, dst_ref=dst, send_sem=send_sem.at[n], recv_sem=recv_sem.at[n],
            device_id=peer, device_id_type=MESH,
        )

    def fill(i, carry):
        for q in range(8):
            r = i * 8 + q
            E[r + 4, 4:36, :] = tok[r].astype(f32)
        return carry

    lax.fori_loop(0, 4, fill, 0)
    near_rows = jnp.where(row_at > 0, 1, 0) + jnp.where(row_at < row_n - 1, 1, 0) + 1
    near_cols = jnp.where(col_at > 0, 1, 0) + jnp.where(col_at < col_n - 1, 1, 0) + 1
    pl.semaphore_wait(barrier, near_rows * near_cols - 1)

    for n, (dr, dc, there, peer) in enumerate(around):

        @pl.when(there)
        def _(n=n, dr=dr, dc=dc, peer=peer):
            copy_to(n, dr, dc, peer).start()

    loads[0].wait()
    loads[1].wait()
    for c in range(6):
        BB[c] = jnp.concatenate([rb[2 * c], rb[2 * c + 1]], axis=1)
    lane = lax.broadcasted_iota(jnp.int32, (64, 128), 1)
    head_of = lane // 32
    for h in range(4):
        ON[h * 64 : (h + 1) * 64] = jnp.where(head_of == h, 1.0, 0.0).astype(bf16)
    low = lane < 64
    qi = lax.broadcasted_iota(jnp.int32, (64, 128), 0)
    kj = lane % 64
    row_cut = (qi // 32) != (kj // 32)
    col_cut = ((qi // 4) % 2) != ((kj // 4) % 2)

    def windows(wi, across):
        first, last = across[0], across[-1]
        count = len(across)
        if count == last - first + 1:
            x = E[pl.ds(wi * 8, 8), first * 8 : (last + 1) * 8, :]
        else:
            x = jnp.concatenate([E[pl.ds(wi * 8, 8), j * 8 : (j + 1) * 8, :] for j in across], axis=1)
        x = norm_rows(x, g1[...].reshape(1, 1, 384))
        m = jnp.concatenate(
            [x[:, n * 8 : (n + 1) * 8, :].reshape(64, 384) for n in range(count)], axis=0
        ).astype(bf16)
        top_row = count * 64
        J[0:top_row, 0:384] = (
            jnp.dot(m, wj[:, 0:384], preferred_element_type=f32) * 32**-0.5
        ).astype(bf16)
        J[0:top_row, 384:1152] = jnp.dot(m, wj[:, 384:1152], preferred_element_type=f32).astype(bf16)
        row_flag = ((wi == 0) & (row_at == 0)) | ((wi == 4) & (row_at == row_n - 1))
        for n, j in enumerate(across):
            cut = row_cut & row_flag
            if j == 0:
                cut = cut | (col_cut & (col_at == 0))
            if j == 4:
                cut = cut | (col_cut & (col_at == col_n - 1))
            sl = slice(n * 64, (n + 1) * 64)
            for g in range(3):
                q = J[sl, g * 128 : (g + 1) * 128]
                k = J[sl, 384 + g * 128 : 384 + (g + 1) * 128]
                v = J[sl, 768 + g * 128 : 768 + (g + 1) * 128]
                kb = jnp.concatenate([k] * 4, axis=0) * ON[...]
                s = lax.dot_general(q, kb, (((1,), (1,)), ((), ())), preferred_element_type=f32)
                es = []
                for c in range(2):
                    b = s[:, c * 128 : (c + 1) * 128] + BB[2 * g + c]
                    b = jnp.where(cut, -1e9, b)
                    m0 = jnp.max(jnp.where(low, b, -3e38), axis=1, keepdims=True)
                    m1 = jnp.max(jnp.where(low, -3e38, b), axis=1, keepdims=True)
                    es.append(jnp.exp(b - jnp.where(low, m0, m1)).astype(bf16))
                p = jnp.concatenate(es, axis=1)
                vb = jnp.concatenate([v] * 4, axis=0) * ON[...]
                o = jnp.dot(p, jnp.concatenate([vb, ON[...]], axis=1), preferred_element_type=f32)
                o = o[:, 0:128] / o[:, 128:256]
                ME[pl.ds(wi * 8, 8), j * 8 : (j + 1) * 8, g * 128 : (g + 1) * 128] = o.reshape(8, 8, 128)

    def inner(n, carry):
        windows(n + 1, (1, 2, 3))
        return carry

    lax.fori_loop(0, 3, inner, 0)

    def land(dr, dc):
        rows = 0 if dr < 0 else 36
        if dc == 0:
            src = top if dr < 0 else bottom
            for r in range(4):
                yield (rows + r, slice(4, 36), lambda r=r: src[r].astype(f32))
            return
        span, part = (slice(0, 4), slice(4, 8)) if dc < 0 else (slice(36, 40), slice(0, 4))
        if dr == 0:
            src = left if dc < 0 else right
            for r in range(32):
                yield (4 + r, span, lambda r=r: src[r].astype(f32)[part])
            return
        piece = corner.at[(0 if dr < 0 else 2) + (0 if dc < 0 else 1)]
        for r in range(4):
            yield (rows + r, span, lambda r=r: piece[r].astype(f32)[part])

    for n, (dr, dc, there, peer) in enumerate(around):

        @pl.when(there)
        def _(n=n, dr=dr, dc=dc, peer=peer):
            copy_to(n, dr, dc, peer).wait_send()
            copy_to(len(around) - 1 - n, -dr, -dc, peer).wait_recv()
            for r, span, value in land(dr, dc):
                E[r, span, :] = value()

        @pl.when(jnp.logical_not(there))
        def _(dr=dr, dc=dc):
            for r, span, value in land(dr, dc):
                E[r, span, :] = jnp.zeros((span.stop - span.start, 384), f32)

    def sides(n, carry):
        windows(n + 1, (0, 4))
        return carry

    lax.fori_loop(0, 3, sides, 0)

    def ends(n, carry):
        windows(n * 4, (0, 1, 2, 3, 4))
        return carry

    lax.fori_loop(0, 2, ends, 0)
    for load in loads[2:]:
        load.wait()
    R = 32

    def tail(c, carry):
        r0 = c * R
        mixed = jnp.concatenate([ME[r0 + q + 4, 4:36, :] for q in range(R)], axis=0).astype(bf16)
        t = jnp.concatenate([tok[r0 + q] for q in range(R)], axis=0).astype(f32)
        res = t + jnp.dot(mixed, wm[...], preferred_element_type=f32)
        n2 = norm_rows(res, g2[...].reshape(1, 384)).astype(bf16)
        h = jnp.dot(n2, we[...], preferred_element_type=f32)
        h = (h * (0.5 + 0.5 * jnp.tanh(h * (G1 + G2 * (h * h))))).astype(bf16)
        b = (res + jnp.dot(h, ws[...], preferred_element_type=f32)).astype(bf16)
        f = jnp.dot(b, wl[...], preferred_element_type=f32).astype(bf16)
        for q in range(R):
            out[r0 + q] = f[q * 32 : (q + 1) * 32]
        return carry

    lax.fori_loop(0, 32 // R, tail, 0)


def swin(tok, g1, g2, wj, wm, we, ws, rb, wl):
    V = pl.BlockSpec(memory_space=pltpu.VMEM)
    A = pl.BlockSpec(memory_space=pl.ANY)
    weights = (wj, wm, we, ws, rb, wl)
    return pl.pallas_call(
        swin_kernel,
        out_shape=jax.ShapeDtypeStruct((32, 32, 256), jnp.bfloat16),
        in_specs=[V] * 3 + [A] * 6,
        out_specs=V,
        scratch_shapes=[pltpu.VMEM(w.shape, w.dtype) for w in weights]
        + [
            pltpu.VMEM((40, 40, 384), jnp.float32),
            pltpu.VMEM((320, 1152), jnp.bfloat16),
            pltpu.VMEM((40, 40, 384), jnp.float32),
            pltpu.VMEM((6, 64, 128), jnp.float32),
            pltpu.VMEM((256, 128), jnp.bfloat16),
            pltpu.VMEM((4, 32, 384), jnp.bfloat16),
            pltpu.VMEM((4, 32, 384), jnp.bfloat16),
            pltpu.VMEM((32, 8, 384), jnp.bfloat16),
            pltpu.VMEM((32, 8, 384), jnp.bfloat16),
            pltpu.VMEM((4, 4, 8, 384), jnp.bfloat16),
            pltpu.SemaphoreType.DMA((8,)),
            pltpu.SemaphoreType.DMA((8,)),
            pltpu.SemaphoreType.DMA((6,)),
        ],
        compiler_params=pltpu.CompilerParams(
            vmem_limit_bytes=63 << 20, collective_id=0, has_side_effects=True
        ),
    )(tok, g1, g2, wj, wm, we, ws, rb, wl)


def gelu_pair(x):
    x2 = x * x
    half = 0.5 + 0.5 * jnp.tanh(x * (G1 + G2 * x2))
    act = x * half
    slope = half + act * (1.0 - half) * (2.0 * G1 + (6.0 * G2) * x2)
    return act, slope


def halves(a):
    hi = a.astype(jnp.bfloat16)
    return hi, (a - hi.astype(jnp.float32)).astype(jnp.bfloat16)


def placement(g, cnt):
    valid = lax.broadcasted_iota(jnp.int32, (16, 1), 0) < cnt
    same = lax.broadcasted_iota(jnp.int32, (16, 16), 0) == lax.broadcasted_iota(
        jnp.int32, (16, 16), 1
    )

    def column(n):
        return jnp.sum(jnp.where(same, g[n : n + 1], 0), axis=1, keepdims=True)

    def rep(col):
        return jnp.concatenate([col] * CROP, axis=0)

    lefts, widths = rep(column(1)), rep(column(3))
    heights = rep(jnp.where(valid, column(2), 0))
    row = lax.broadcasted_iota(jnp.int32, (ROWS, 1), 0)
    vv, kk = row // 16, row % 16
    in_w = vv < widths
    target = jnp.where(in_w, kk * 32 + lefts + vv, -1)
    lane = lax.broadcasted_iota(jnp.int32, (ROWS, 512), 1)
    pick = jnp.where(lane == target, 1.0, 0.0).astype(jnp.bfloat16)
    return pick, in_w, heights


def mask_kernel(gs, cs, geom, own, soft, feat, w_h, mw, G, out, A, T, D, tgt, lg, w, V, P, rt, recv, sem, send_sem, recv_sem):
    f32, bf16 = jnp.float32, jnp.bfloat16
    cnt = cs[0, 0]
    loads = [pltpu.make_async_copy(w_h.at[n], w.at[n], sem.at[n]) for n in range(4)]
    for load in loads:
        load.start()
    me, n_row = lax.axis_index("row"), lax.axis_size("row")
    col_at = lax.axis_index("col")
    barrier = pltpu.get_barrier_semaphore()
    for d in range(1, 16):
        pl.semaphore_signal(
            barrier, inc=1, device_id=(lax.rem(me + d, n_row), col_at), device_id_type=MESH
        )

    def copy_to(d, slot):
        peer = lax.rem(me + d, n_row)
        return pltpu.make_async_remote_copy(
            src_ref=rt.at[peer], dst_ref=recv.at[slot],
            send_sem=send_sem.at[d], recv_sem=recv_sem.at[d],
            device_id=(peer, col_at), device_id_type=MESH,
        )

    zrow = jnp.zeros((256, 256), bf16)
    A[0] = zrow
    A[15] = zrow
    for u in range(1, 15):
        A[u, 0:16, :] = zrow[0:16]
        A[u, 240:256, :] = zrow[0:16]
    pick, in_w, heights = placement(geom[0, 0], cnt)
    soft_rows = soft[0, 0]
    cell = lax.broadcasted_iota(jnp.int32, (CROP * CROP, 128), 0)
    step = lax.broadcasted_iota(jnp.int32, (CROP * CROP, 128), 1)
    for v in range(CROP):
        spread = jnp.where(cell == step * CROP + v, 1.0, 0.0).astype(bf16)
        tgt[v * 16 : (v + 1) * 16] = jnp.dot(soft_rows, spread, preferred_element_type=f32)

    def gather(i, c):
        for q in range(2):
            u = 2 * i + q
            strips = jnp.concatenate([feat[gs[0, 0, 0, k] + u] for k in range(16)], axis=0)
            crop = jnp.dot(pick, strips, preferred_element_type=f32)
            crop = jnp.where(u < heights, crop, 0.0)
            A[u + 1, 16:240, :] = crop.astype(bf16)
        return c

    lax.fori_loop(0, CROP // 2, gather, 0)
    lg[...] = jnp.zeros_like(lg)

    def form(j):
        for m in range(7):
            d = [A[2 * m + i] for i in range(4)]
            T[j, m] = (d[0] - d[2], d[1] + d[2], d[2] - d[1], d[1] - d[3])[j]

    def taps(l):
        for n in range(0, 768, 256):
            a = w[l, n : n + 256].astype(f32) + w[l, 1536 + n : 1792 + n].astype(f32)
            b = w[l, 768 + n : 1024 + n].astype(f32)
            V[l, 0, n : n + 256] = (0.5 * (a + b)).astype(bf16)
            V[l, 1, n : n + 256] = (0.5 * (a - b)).astype(bf16)

    def kernel_of(l, j):
        return (w.at[l, 0:768], V.at[l, 0], V.at[l, 1], w.at[l, 1536:2304])[j]

    def shifted(j, t):
        return jnp.concatenate([T[j, m, t * 16 : t * 16 + ROWS, :] for m in range(7)], axis=0)

    def fwd_product(l, j):
        lhs = jnp.concatenate([shifted(j, t) for t in range(3)], axis=1)
        return jnp.dot(lhs, kernel_of(l, j)[...], preferred_element_type=f32)

    def bwd_product(l, j):
        ref = kernel_of(l, 3 - j if j in (0, 3) else j)
        acc = None
        for t in range(3):
            d = lax.dot_general(
                shifted(j, 2 - t), ref[t * 256 : (t + 1) * 256], (((1,), (1,)), ((), ())),
                preferred_element_type=f32,
            )
            acc = d if acc is None else acc + d
        return acc

    def finish_fwd(l, u, pre):
        act, slope = gelu_pair(pre)
        A[u + 1, 16:240, :] = act.astype(bf16)
        D[l, u] = slope.astype(bf16)

    def finish_last(l, u, pre):
        act, slope = gelu_pair(pre)
        m = mw[...].astype(f32).reshape(1, 256)
        logit = jnp.sum(act.astype(bf16).astype(f32) * m, axis=1, keepdims=True)
        sel = lax.broadcasted_iota(jnp.int32, (ROWS, 128), 1) == u
        lg[...] = jnp.where(sel, logit, lg[...])
        tg = tgt[:, u : u + 1]
        gl = jnp.where(in_w & (u < heights), 128.0 * (jax.nn.sigmoid(logit) - tg), 0.0)
        A[u + 1, 16:240, :] = (gl * m * slope).astype(bf16)

    def layer(l, product, finish, first, waiting, parity):
        lead = 3 if first == 0 else 0
        rest = 3 - lead
        p1, p2, p_lead, p_rest = P.at[0], P.at[1], P.at[2 + parity], P.at[4 + parity]
        form(lead)
        p_lead[...] = product(l, lead)
        waiting()
        for j in (1, 2, rest):
            form(j)
        p1[...] = product(l, 1)
        p2[...] = product(l, 2)
        p_rest[...] = product(l, rest)

        def done(odd, edge):
            for m in range(7):
                sl = slice(m * ROWS, (m + 1) * ROWS)
                x = p1[sl] - p2[sl] - edge[sl] if odd else p1[sl] + p2[sl] + edge[sl]
                finish(l, 2 * m + odd, x)

        other = 1 - first
        done(other, p_lead)
        return other, lambda: done(first, p_rest), 1 - parity

    loads[0].wait()
    taps(0)
    state = (0, lambda: None, 0)
    for l in range(4):
        state = layer(l, fwd_product, finish_last if l == 3 else finish_fwd, *state)
        if l < 3:
            loads[l + 1].wait()
            taps(l + 1)
    state[1]()

    def products(l):
        for j in range(4):
            form(j)
        for j in range(4):
            P[j] = bwd_product(l, j)

    def rows_of(m, odd):
        sl = slice(m * ROWS, (m + 1) * ROWS)
        return P[1, sl] - P[2, sl] - P[3, sl] if odd else P[0, sl] + P[1, sl] + P[2, sl]

    spot = lax.broadcasted_iota(jnp.int32, (128, 256), 1)
    from_u = lax.broadcasted_iota(jnp.int32, (128, 256), 0)
    flat = jnp.zeros((16, 256), f32)
    for v in range(CROP):
        spread = jnp.where((spot == from_u * CROP + v) & (from_u < CROP), 1.0, 0.0).astype(bf16)
        for part in halves(lg[v * 16 : (v + 1) * 16]):
            flat = flat + jnp.dot(part, spread, preferred_element_type=f32)
    flat = jnp.where(lax.broadcasted_iota(jnp.int32, (16, 256), 1) < CROP * CROP, flat, 1.0)
    used = lax.broadcasted_iota(jnp.int32, (16, 16), 1) < cnt
    sent = (own[0] == lax.broadcasted_iota(jnp.int32, (16, 16), 0)) & used
    sent = jnp.where(sent, 1.0, 0.0).astype(bf16)
    routed = jnp.zeros((16, 256), f32)
    for part in halves(flat):
        routed = routed + jnp.dot(sent, part, preferred_element_type=f32)
    for o in range(16):
        rt[o] = routed[o : o + 1]
    recv[me] = rt[me]
    pl.semaphore_wait(barrier, 15)

    def back(i, c):
        l = 3 - i

        @pl.when(i == 1)
        def _():
            for d in range(1, 16):
                copy_to(d, me).start()

        products(l)
        for u in range(CROP):
            A[u + 1, 16:240, :] = (rows_of(u // 2, u % 2) * D[l - 1, u].astype(f32)).astype(bf16)
        return c

    lax.fori_loop(0, 3, back, 0)
    products(0)
    for u in range(CROP):
        G[u] = jnp.where(u < heights, rows_of(u // 2, u % 2), 0.0).astype(bf16)

    for d in range(1, 16):
        copy_to(d, lax.rem(me + n_row - d, n_row)).wait()
    got = jnp.concatenate([recv[i] for i in range(16)], axis=0)
    flag = jnp.where(got[:, 255:256] > 0.5, 1.0, 0.0)
    later = lax.broadcasted_iota(jnp.int32, (16, 16), 0) > lax.broadcasted_iota(
        jnp.int32, (16, 16), 1
    )
    place = jnp.dot(
        jnp.where(later, 1.0, 0.0).astype(bf16),
        jnp.broadcast_to(flag, (16, 128)).astype(bf16),
        preferred_element_type=f32,
    )[:, 0:1]
    rows = [
        jnp.sum(jnp.where((place == float(i)) & (flag > 0.5), got, 0.0), axis=0, keepdims=True)
        for i in range(BOX_OWN)
    ]
    out[0, 0] = jnp.concatenate(rows, axis=0)[:, 0 : CROP * CROP]


def place_kernel(gs, cs, geom, G, logits, feat, fg, logits_out, feat_out, PT, sem):
    load = pltpu.make_async_copy(feat, feat_out, sem.at[0])
    load.start()
    pick, _, _ = placement(geom[0, 0], cs[0, 0])
    PT[...] = pick.astype(jnp.float32).T.astype(jnp.bfloat16)
    logits_out[...] = logits[...]
    fg[...] = jnp.zeros_like(fg)

    def put(i, c):
        for q in range(2):
            u = 2 * i + q
            z = jnp.dot(PT[...], G[u], preferred_element_type=jnp.float32)
            for k in range(16):
                fg[gs[0, 0, 0, k] + u] += z[k * 32 : (k + 1) * 32]
        return c

    lax.fori_loop(0, CROP // 2, put, 0)
    load.wait()


def mask_head(geometry, count, owner, soft, feat, conv_w, mask_w):
    V = pl.BlockSpec(memory_space=pltpu.VMEM)
    S = pl.BlockSpec(memory_space=pltpu.SMEM)
    H = pl.BlockSpec(memory_space=pl.ANY)
    grads, logits = pl.pallas_call(
        mask_kernel,
        out_shape=(
            jax.ShapeDtypeStruct((CROP, ROWS, 256), jnp.bfloat16),
            jax.ShapeDtypeStruct((1, 1, BOX_OWN, CROP * CROP), jnp.float32),
        ),
        in_specs=[S, S, V, V, V, V, H, V],
        out_specs=(V, V),
        scratch_shapes=[
            pltpu.VMEM((16, 256, 256), jnp.bfloat16),
            pltpu.VMEM((4, 7, 256, 256), jnp.bfloat16),
            pltpu.VMEM((3, 14, ROWS, 256), jnp.bfloat16),
            pltpu.VMEM((ROWS, 128), jnp.float32),
            pltpu.VMEM((ROWS, 128), jnp.float32),
            pltpu.VMEM((4, 2304, 256), jnp.bfloat16),
            pltpu.VMEM((4, 2, 768, 256), jnp.bfloat16),
            pltpu.VMEM((6, 7 * ROWS, 256), jnp.float32),
            pltpu.VMEM((16, 1, 256), jnp.float32),
            pltpu.VMEM((16, 1, 256), jnp.float32),
            pltpu.SemaphoreType.DMA((4,)),
            pltpu.SemaphoreType.DMA((16,)),
            pltpu.SemaphoreType.DMA((16,)),
        ],
        compiler_params=pltpu.CompilerParams(
            vmem_limit_bytes=63 << 20, collective_id=1, has_side_effects=True
        ),
    )(geometry, count, geometry, owner, soft, feat, conv_w, mask_w)
    return pl.pallas_call(
        place_kernel,
        out_shape=(
            jax.ShapeDtypeStruct((32, 32, 256), jnp.float32),
            jax.ShapeDtypeStruct((1, 1, BOX_OWN, CROP * CROP), jnp.float32),
            jax.ShapeDtypeStruct((32, 32, 256), jnp.bfloat16),
        ),
        in_specs=[S, S, V, V, V, V],
        out_specs=(V, V, H),
        scratch_shapes=[pltpu.VMEM((512, ROWS), jnp.bfloat16), pltpu.SemaphoreType.DMA((1,))],
        compiler_params=pltpu.CompilerParams(vmem_limit_bytes=63 << 20),
    )(geometry, count, geometry, grads, logits, feat)


def shards(
    tokens,
    first_gain,
    second_gain,
    joint_weight,
    merge_weight,
    expand_weight,
    shrink_weight,
    relative_bias,
    lateral_weight,
    conv_weight,
    mask_weight,
    box_geometry,
    box_counts,
    box_owner,
    soft_target,
):
    features = swin(
        tokens, first_gain, second_gain, joint_weight, merge_weight,
        expand_weight, shrink_weight, relative_bias, lateral_weight,
    )
    feature_grad, logits, features = mask_head(
        box_geometry.transpose(0, 1, 3, 2), box_counts, box_owner, soft_target, features,
        conv_weight, mask_weight,
    )
    return (features, feature_grad, logits)


def solution(mesh):
    placed = (
        P("row", "col", None),
        P(),
        P(),
        P(),
        P(),
        P(),
        P(),
        P(),
        P(),
        P(),
        P(),
        P("row", "col", None, None),
        P("row", "col"),
        P("row", "col", None),
        P("row", "col", None, None),
    )
    return jax.shard_map(
        shards,
        mesh=mesh,
        in_specs=placed,
        out_specs=(P("row", "col", None), P("row", "col", None), P("row", "col", None, None)),
        check_vma=False,
    )
```

```python
import functools
import jax
import jax.numpy as jnp
from jax import lax
from jax.experimental import pallas as pl
from jax.experimental.pallas import tpu as pltpu
from jax.sharding import PartitionSpec as P

CROP = 14
BOX_OWN = 8
EPSILON = 1e-05
G1 = 0.7978845608028654
G2 = G1 * 0.044715
ROWS = 224
MESH = pl.DeviceIdType.MESH


def norm_rows(x, gain):
    x = x - jnp.mean(x, axis=-1, keepdims=True)
    return x * lax.rsqrt(jnp.mean(x * x, axis=-1, keepdims=True) + EPSILON) * gain


def neighbours():
    row_at, row_n = lax.axis_index("row"), lax.axis_size("row")
    col_at, col_n = lax.axis_index("col"), lax.axis_size("col")
    found = []
    for dr in (-1, 0, 1):
        for dc in (-1, 0, 1):
            if dr == 0 and dc == 0:
                continue
            there = None
            for d, at, n in ((dr, row_at, row_n), (dc, col_at, col_n)):
                if d:
                    ok = at > 0 if d < 0 else at < n - 1
                    there = ok if there is None else there & ok
            found.append((dr, dc, there, (row_at + dr, col_at + dc)))
    return found


def swin_kernel(
    tok, g1, g2, wj_h, wm_h, we_h, ws_h, rb_h, wl_h, out,
    wj, wm, we, ws, rb, wl, E, J, ME, BB, ON,
    top, bottom, left, right, corner, send_sem, recv_sem, load_sem,
):
    f32, bf16 = jnp.float32, jnp.bfloat16
    row_at, row_n = lax.axis_index("row"), lax.axis_size("row")
    col_at, col_n = lax.axis_index("col"), lax.axis_size("col")
    loads = [
        pltpu.make_async_copy(src, dst, load_sem.at[n])
        for n, (src, dst) in enumerate(
            ((wj_h, wj), (rb_h, rb), (wm_h, wm), (we_h, we), (ws_h, ws), (wl_h, wl))
        )
    ]
    for load in loads:
        load.start()
    around = neighbours()
    barrier = pltpu.get_barrier_semaphore()
    for dr, dc, there, peer in around:

        @pl.when(there)
        def _(peer=peer):
            pl.semaphore_signal(barrier, inc=1, device_id=peer, device_id_type=MESH)

    def parts(dr, dc):
        if dc == 0:
            return (tok.at[0:4], bottom) if dr < 0 else (tok.at[28:32], top)
        span = slice(0, 8) if dc < 0 else slice(24, 32)
        if dr == 0:
            return tok.at[:, span], (right if dc < 0 else left)
        piece = tok.at[0:4, span] if dr < 0 else tok.at[28:32, span]
        return piece, corner.at[(0 if dr > 0 else 2) + (0 if dc > 0 else 1)]

    def copy_to(n, dr, dc, peer):
        src, dst = parts(dr, dc)
        return pltpu.make_async_remote_copy(
            src_ref=src, dst_ref=dst, send_sem=send_sem.at[n], recv_sem=recv_sem.at[n],
            device_id=peer, device_id_type=MESH,
        )

    def fill(i, carry):
        for q in range(8):
            r = i * 8 + q
            E[r + 4, 4:36, :] = tok[r].astype(f32)
        return carry

    lax.fori_loop(0, 4, fill, 0)
    near_rows = jnp.where(row_at > 0, 1, 0) + jnp.where(row_at < row_n - 1, 1, 0) + 1
    near_cols = jnp.where(col_at > 0, 1, 0) + jnp.where(col_at < col_n - 1, 1, 0) + 1
    pl.semaphore_wait(barrier, near_rows * near_cols - 1)

    for n, (dr, dc, there, peer) in enumerate(around):

        @pl.when(there)
        def _(n=n, dr=dr, dc=dc, peer=peer):
            copy_to(n, dr, dc, peer).start()

    loads[0].wait()
    loads[1].wait()
    for c in range(6):
        BB[c] = jnp.concatenate([rb[2 * c], rb[2 * c + 1]], axis=1)
    lane = lax.broadcasted_iota(jnp.int32, (64, 128), 1)
    head_of = lane // 32
    for h in range(4):
        ON[h * 64 : (h + 1) * 64] = jnp.where(head_of == h, 1.0, 0.0).astype(bf16)
    low = lane < 64
    qi = lax.broadcasted_iota(jnp.int32, (64, 128), 0)
    kj = lane % 64
    row_cut = (qi // 32) != (kj // 32)
    col_cut = ((qi // 4) % 2) != ((kj // 4) % 2)

    def windows(wi, across):
        first, last = across[0], across[-1]
        count = len(across)
        if count == last - first + 1:
            x = E[pl.ds(wi * 8, 8), first * 8 : (last + 1) * 8, :]
        else:
            x = jnp.concatenate([E[pl.ds(wi * 8, 8), j * 8 : (j + 1) * 8, :] for j in across], axis=1)
        x = norm_rows(x, g1[...].reshape(1, 1, 384))
        m = jnp.concatenate(
            [x[:, n * 8 : (n + 1) * 8, :].reshape(64, 384) for n in range(count)], axis=0
        ).astype(bf16)
        top_row = count * 64
        J[0:top_row, 0:384] = (
            jnp.dot(m, wj[:, 0:384], preferred_element_type=f32) * 32**-0.5
        ).astype(bf16)
        J[0:top_row, 384:1152] = jnp.dot(m, wj[:, 384:1152], preferred_element_type=f32).astype(bf16)
        row_flag = ((wi == 0) & (row_at == 0)) | ((wi == 4) & (row_at == row_n - 1))
        for n, j in enumerate(across):
            cut = row_cut & row_flag
            if j == 0:
                cut = cut | (col_cut & (col_at == 0))
            if j == 4:
                cut = cut | (col_cut & (col_at == col_n - 1))
            sl = slice(n * 64, (n + 1) * 64)
            for g in range(3):
                q = J[sl, g * 128 : (g + 1) * 128]
                k = J[sl, 384 + g * 128 : 384 + (g + 1) * 128]
                v = J[sl, 768 + g * 128 : 768 + (g + 1) * 128]
                kb = jnp.concatenate([k] * 4, axis=0) * ON[...]
                s = lax.dot_general(q, kb, (((1,), (1,)), ((), ())), preferred_element_type=f32)
                es = []
                for c in range(2):
                    b = s[:, c * 128 : (c + 1) * 128] + BB[2 * g + c]
                    b = jnp.where(cut, -1e9, b)
                    m0 = jnp.max(jnp.where(low, b, -3e38), axis=1, keepdims=True)
                    m1 = jnp.max(jnp.where(low, -3e38, b), axis=1, keepdims=True)
                    es.append(jnp.exp(b - jnp.where(low, m0, m1)).astype(bf16))
                p = jnp.concatenate(es, axis=1)
                vb = jnp.concatenate([v] * 4, axis=0) * ON[...]
                o = jnp.dot(p, jnp.concatenate([vb, ON[...]], axis=1), preferred_element_type=f32)
                o = o[:, 0:128] / o[:, 128:256]
                ME[pl.ds(wi * 8, 8), j * 8 : (j + 1) * 8, g * 128 : (g + 1) * 128] = o.reshape(8, 8, 128)

    def inner(n, carry):
        windows(n + 1, (1, 2, 3))
        return carry

    lax.fori_loop(0, 3, inner, 0)

    def land(dr, dc):
        rows = 0 if dr < 0 else 36
        if dc == 0:
            src = top if dr < 0 else bottom
            for r in range(4):
                yield (rows + r, slice(4, 36), lambda r=r: src[r].astype(f32))
            return
        span, part = (slice(0, 4), slice(4, 8)) if dc < 0 else (slice(36, 40), slice(0, 4))
        if dr == 0:
            src = left if dc < 0 else right
            for r in range(32):
                yield (4 + r, span, lambda r=r: src[r].astype(f32)[part])
            return
        piece = corner.at[(0 if dr < 0 else 2) + (0 if dc < 0 else 1)]
        for r in range(4):
            yield (rows + r, span, lambda r=r: piece[r].astype(f32)[part])

    for n, (dr, dc, there, peer) in enumerate(around):

        @pl.when(there)
        def _(n=n, dr=dr, dc=dc, peer=peer):
            copy_to(n, dr, dc, peer).wait_send()
            copy_to(len(around) - 1 - n, -dr, -dc, peer).wait_recv()
            for r, span, value in land(dr, dc):
                E[r, span, :] = value()

        @pl.when(jnp.logical_not(there))
        def _(dr=dr, dc=dc):
            for r, span, value in land(dr, dc):
                E[r, span, :] = jnp.zeros((span.stop - span.start, 384), f32)

    def sides(n, carry):
        windows(n + 1, (0, 4))
        return carry

    lax.fori_loop(0, 3, sides, 0, unroll=True)

    def ends(n, carry):
        windows(n * 4, (0, 1, 2, 3, 4))
        return carry

    lax.fori_loop(0, 2, ends, 0)
    for load in loads[2:]:
        load.wait()
    R = 32

    def tail(c, carry):
        r0 = c * R
        mixed = jnp.concatenate([ME[r0 + q + 4, 4:36, :] for q in range(R)], axis=0).astype(bf16)
        t = jnp.concatenate([tok[r0 + q] for q in range(R)], axis=0).astype(f32)
        res = t + jnp.dot(mixed, wm[...], preferred_element_type=f32)
        n2 = norm_rows(res, g2[...].reshape(1, 384)).astype(bf16)
        h = jnp.dot(n2, we[...], preferred_element_type=f32)
        h = (h * (0.5 + 0.5 * jnp.tanh(h * (G1 + G2 * (h * h))))).astype(bf16)
        b = (res + jnp.dot(h, ws[...], preferred_element_type=f32)).astype(bf16)
        f = jnp.dot(b, wl[...], preferred_element_type=f32).astype(bf16)
        for q in range(R):
            out[r0 + q] = f[q * 32 : (q + 1) * 32]
        return carry

    lax.fori_loop(0, 32 // R, tail, 0)


def swin(tok, g1, g2, wj, wm, we, ws, rb, wl):
    V = pl.BlockSpec(memory_space=pltpu.VMEM)
    A = pl.BlockSpec(memory_space=pl.ANY)
    weights = (wj, wm, we, ws, rb, wl)
    return pl.pallas_call(
        swin_kernel,
        out_shape=jax.ShapeDtypeStruct((32, 32, 256), jnp.bfloat16),
        in_specs=[V] * 3 + [A] * 6,
        out_specs=V,
        scratch_shapes=[pltpu.VMEM(w.shape, w.dtype) for w in weights]
        + [
            pltpu.VMEM((40, 40, 384), jnp.float32),
            pltpu.VMEM((320, 1152), jnp.bfloat16),
            pltpu.VMEM((40, 40, 384), jnp.float32),
            pltpu.VMEM((6, 64, 128), jnp.float32),
            pltpu.VMEM((256, 128), jnp.bfloat16),
            pltpu.VMEM((4, 32, 384), jnp.bfloat16),
            pltpu.VMEM((4, 32, 384), jnp.bfloat16),
            pltpu.VMEM((32, 8, 384), jnp.bfloat16),
            pltpu.VMEM((32, 8, 384), jnp.bfloat16),
            pltpu.VMEM((4, 4, 8, 384), jnp.bfloat16),
            pltpu.SemaphoreType.DMA((8,)),
            pltpu.SemaphoreType.DMA((8,)),
            pltpu.SemaphoreType.DMA((6,)),
        ],
        compiler_params=pltpu.CompilerParams(
            vmem_limit_bytes=63 << 20, collective_id=0, has_side_effects=True
        ),
    )(tok, g1, g2, wj, wm, we, ws, rb, wl)


def gelu_pair(x):
    x2 = x * x
    half = 0.5 + 0.5 * jnp.tanh(x * (G1 + G2 * x2))
    act = x * half
    slope = half + act * (1.0 - half) * (2.0 * G1 + (6.0 * G2) * x2)
    return act, slope


def halves(a):
    hi = a.astype(jnp.bfloat16)
    return hi, (a - hi.astype(jnp.float32)).astype(jnp.bfloat16)


def placement(g, cnt):
    valid = lax.broadcasted_iota(jnp.int32, (16, 1), 0) < cnt
    same = lax.broadcasted_iota(jnp.int32, (16, 16), 0) == lax.broadcasted_iota(
        jnp.int32, (16, 16), 1
    )

    def column(n):
        return jnp.sum(jnp.where(same, g[n : n + 1], 0), axis=1, keepdims=True)

    def rep(col):
        return jnp.concatenate([col] * CROP, axis=0)

    lefts, widths = rep(column(1)), rep(column(3))
    heights = rep(jnp.where(valid, column(2), 0))
    row = lax.broadcasted_iota(jnp.int32, (ROWS, 1), 0)
    vv, kk = row // 16, row % 16
    in_w = vv < widths
    target = jnp.where(in_w, kk * 32 + lefts + vv, -1)
    lane = lax.broadcasted_iota(jnp.int32, (ROWS, 512), 1)
    pick = jnp.where(lane == target, 1.0, 0.0).astype(jnp.bfloat16)
    return pick, in_w, heights


def mask_kernel(gs, cs, geom, own, soft, feat, w_h, mw, G, out, A, T, D, tgt, lg, w, V, P, rt, recv, sem, send_sem, recv_sem):
    f32, bf16 = jnp.float32, jnp.bfloat16
    cnt = cs[0, 0]
    loads = [pltpu.make_async_copy(w_h.at[n], w.at[n], sem.at[n]) for n in range(4)]
    for load in loads:
        load.start()
    me, n_row = lax.axis_index("row"), lax.axis_size("row")
    col_at = lax.axis_index("col")
    barrier = pltpu.get_barrier_semaphore()
    for d in range(1, 16):
        pl.semaphore_signal(
            barrier, inc=1, device_id=(lax.rem(me + d, n_row), col_at), device_id_type=MESH
        )

    def copy_to(d, slot):
        peer = lax.rem(me + d, n_row)
        return pltpu.make_async_remote_copy(
            src_ref=rt.at[peer], dst_ref=recv.at[slot],
            send_sem=send_sem.at[d], recv_sem=recv_sem.at[d],
            device_id=(peer, col_at), device_id_type=MESH,
        )

    zrow = jnp.zeros((256, 256), bf16)
    A[0] = zrow
    A[15] = zrow
    for u in range(1, 15):
        A[u, 0:16, :] = zrow[0:16]
        A[u, 240:256, :] = zrow[0:16]
    pick, in_w, heights = placement(geom[0, 0], cnt)
    soft_rows = soft[0, 0]
    cell = lax.broadcasted_iota(jnp.int32, (CROP * CROP, 128), 0)
    step = lax.broadcasted_iota(jnp.int32, (CROP * CROP, 128), 1)
    for v in range(CROP):
        spread = jnp.where(cell == step * CROP + v, 1.0, 0.0).astype(bf16)
        tgt[v * 16 : (v + 1) * 16] = jnp.dot(soft_rows, spread, preferred_element_type=f32)

    def gather(i, c):
        for q in range(7):
            u = 7 * i + q
            strips = jnp.concatenate([feat[gs[0, 0, 0, k] + u] for k in range(16)], axis=0)
            crop = jnp.dot(pick, strips, preferred_element_type=f32)
            crop = jnp.where(u < heights, crop, 0.0)
            A[u + 1, 16:240, :] = crop.astype(bf16)
        return c

    lax.fori_loop(0, CROP // 7, gather, 0)
    lg[...] = jnp.zeros_like(lg)

    def form(j):
        for m in range(7):
            d = [A[2 * m + i] for i in range(4)]
            T[j, m] = (d[0] - d[2], d[1] + d[2], d[2] - d[1], d[1] - d[3])[j]

    def taps(l):
        for n in range(0, 768, 256):
            a = w[l, n : n + 256].astype(f32) + w[l, 1536 + n : 1792 + n].astype(f32)
            b = w[l, 768 + n : 1024 + n].astype(f32)
            V[l, 0, n : n + 256] = (0.5 * (a + b)).astype(bf16)
            V[l, 1, n : n + 256] = (0.5 * (a - b)).astype(bf16)

    def kernel_of(l, j):
        return (w.at[l, 0:768], V.at[l, 0], V.at[l, 1], w.at[l, 1536:2304])[j]

    def shifted(j, t):
        return jnp.concatenate([T[j, m, t * 16 : t * 16 + ROWS, :] for m in range(7)], axis=0)

    def fwd_product(l, j):
        lhs = jnp.concatenate([shifted(j, t) for t in range(3)], axis=1)
        return jnp.dot(lhs, kernel_of(l, j)[...], preferred_element_type=f32)

    def bwd_product(l, j):
        ref = kernel_of(l, 3 - j if j in (0, 3) else j)
        acc = None
        for t in range(3):
            d = lax.dot_general(
                shifted(j, 2 - t), ref[t * 256 : (t + 1) * 256], (((1,), (1,)), ((), ())),
                preferred_element_type=f32,
            )
            acc = d if acc is None else acc + d
        return acc

    def finish_fwd(l, u, pre):
        act, slope = gelu_pair(pre)
        A[u + 1, 16:240, :] = act.astype(bf16)
        D[l, u] = slope.astype(bf16)

    def finish_last(l, u, pre):
        act, slope = gelu_pair(pre)
        m = mw[...].astype(f32).reshape(1, 256)
        logit = jnp.sum(act.astype(bf16).astype(f32) * m, axis=1, keepdims=True)
        sel = lax.broadcasted_iota(jnp.int32, (ROWS, 128), 1) == u
        lg[...] = jnp.where(sel, logit, lg[...])
        tg = tgt[:, u : u + 1]
        gl = jnp.where(in_w & (u < heights), 128.0 * (jax.nn.sigmoid(logit) - tg), 0.0)
        A[u + 1, 16:240, :] = (gl * m * slope).astype(bf16)

    def layer(l, product, finish, first, waiting, parity):
        lead = 3 if first == 0 else 0
        rest = 3 - lead
        p1, p2, p_lead, p_rest = P.at[0], P.at[1], P.at[2 + parity], P.at[4 + parity]
        form(lead)
        p_lead[...] = product(l, lead)
        waiting()
        for j in (1, 2, rest):
            form(j)
        p1[...] = product(l, 1)
        p2[...] = product(l, 2)
        p_rest[...] = product(l, rest)

        def done(odd, edge):
            for m in range(7):
                sl = slice(m * ROWS, (m + 1) * ROWS)
                x = p1[sl] - p2[sl] - edge[sl] if odd else p1[sl] + p2[sl] + edge[sl]
                finish(l, 2 * m + odd, x)

        other = 1 - first
        done(other, p_lead)
        return other, lambda: done(first, p_rest), 1 - parity

    loads[0].wait()
    taps(0)
    state = (0, lambda: None, 0)
    for l in range(4):
        state = layer(l, fwd_product, finish_last if l == 3 else finish_fwd, *state)
        if l < 3:
            loads[l + 1].wait()
            taps(l + 1)
    state[1]()

    def products(l):
        for j in range(4):
            form(j)
        for j in range(4):
            P[j] = bwd_product(l, j)

    def rows_of(m, odd):
        sl = slice(m * ROWS, (m + 1) * ROWS)
        return P[1, sl] - P[2, sl] - P[3, sl] if odd else P[0, sl] + P[1, sl] + P[2, sl]

    spot = lax.broadcasted_iota(jnp.int32, (128, 256), 1)
    from_u = lax.broadcasted_iota(jnp.int32, (128, 256), 0)
    flat = jnp.zeros((16, 256), f32)
    for v in range(CROP):
        spread = jnp.where((spot == from_u * CROP + v) & (from_u < CROP), 1.0, 0.0).astype(bf16)
        for part in halves(lg[v * 16 : (v + 1) * 16]):
            flat = flat + jnp.dot(part, spread, preferred_element_type=f32)
    flat = jnp.where(lax.broadcasted_iota(jnp.int32, (16, 256), 1) < CROP * CROP, flat, 1.0)
    used = lax.broadcasted_iota(jnp.int32, (16, 16), 1) < cnt
    sent = (own[0] == lax.broadcasted_iota(jnp.int32, (16, 16), 0)) & used
    sent = jnp.where(sent, 1.0, 0.0).astype(bf16)
    routed = jnp.zeros((16, 256), f32)
    for part in halves(flat):
        routed = routed + jnp.dot(sent, part, preferred_element_type=f32)
    for o in range(16):
        rt[o] = routed[o : o + 1]
    recv[me] = rt[me]
    pl.semaphore_wait(barrier, 15)

    def back(i, c):
        l = 3 - i

        @pl.when(i == 1)
        def _():
            for d in range(1, 16):
                copy_to(d, me).start()

        products(l)
        for u in range(CROP):
            A[u + 1, 16:240, :] = (rows_of(u // 2, u % 2) * D[l - 1, u].astype(f32)).astype(bf16)
        return c

    lax.fori_loop(0, 3, back, 0)
    products(0)
    for u in range(CROP):
        G[u] = jnp.where(u < heights, rows_of(u // 2, u % 2), 0.0).astype(bf16)

    for d in range(1, 16):
        copy_to(d, lax.rem(me + n_row - d, n_row)).wait()
    got = jnp.concatenate([recv[i] for i in range(16)], axis=0)
    flag = jnp.where(got[:, 255:256] > 0.5, 1.0, 0.0)
    later = lax.broadcasted_iota(jnp.int32, (16, 16), 0) > lax.broadcasted_iota(
        jnp.int32, (16, 16), 1
    )
    place = jnp.dot(
        jnp.where(later, 1.0, 0.0).astype(bf16),
        jnp.broadcast_to(flag, (16, 128)).astype(bf16),
        preferred_element_type=f32,
    )[:, 0:1]
    rows = [
        jnp.sum(jnp.where((place == float(i)) & (flag > 0.5), got, 0.0), axis=0, keepdims=True)
        for i in range(BOX_OWN)
    ]
    out[0, 0] = jnp.concatenate(rows, axis=0)[:, 0 : CROP * CROP]


def place_kernel(gs, cs, geom, G, logits, feat, fg, logits_out, feat_out, PT, sem):
    load = pltpu.make_async_copy(feat, feat_out, sem.at[0])
    load.start()
    pick, _, _ = placement(geom[0, 0], cs[0, 0])
    PT[...] = pick.astype(jnp.float32).T.astype(jnp.bfloat16)
    logits_out[...] = logits[...]
    fg[...] = jnp.zeros_like(fg)

    def put(i, c):
        for q in range(7):
            u = 7 * i + q
            z = jnp.dot(PT[...], G[u], preferred_element_type=jnp.float32)
            for k in range(16):
                fg[gs[0, 0, 0, k] + u] += z[k * 32 : (k + 1) * 32]
        return c

    lax.fori_loop(0, CROP // 7, put, 0)
    load.wait()


def mask_head(geometry, count, owner, soft, feat, conv_w, mask_w):
    V = pl.BlockSpec(memory_space=pltpu.VMEM)
    S = pl.BlockSpec(memory_space=pltpu.SMEM)
    H = pl.BlockSpec(memory_space=pl.ANY)
    grads, logits = pl.pallas_call(
        mask_kernel,
        out_shape=(
            jax.ShapeDtypeStruct((CROP, ROWS, 256), jnp.bfloat16),
            jax.ShapeDtypeStruct((1, 1, BOX_OWN, CROP * CROP), jnp.float32),
        ),
        in_specs=[S, S, V, V, V, V, H, V],
        out_specs=(V, V),
        scratch_shapes=[
            pltpu.VMEM((16, 256, 256), jnp.bfloat16),
            pltpu.VMEM((4, 7, 256, 256), jnp.bfloat16),
            pltpu.VMEM((3, 14, ROWS, 256), jnp.bfloat16),
            pltpu.VMEM((ROWS, 128), jnp.float32),
            pltpu.VMEM((ROWS, 128), jnp.float32),
            pltpu.VMEM((4, 2304, 256), jnp.bfloat16),
            pltpu.VMEM((4, 2, 768, 256), jnp.bfloat16),
            pltpu.VMEM((6, 7 * ROWS, 256), jnp.float32),
            pltpu.VMEM((16, 1, 256), jnp.float32),
            pltpu.VMEM((16, 1, 256), jnp.float32),
            pltpu.SemaphoreType.DMA((4,)),
            pltpu.SemaphoreType.DMA((16,)),
            pltpu.SemaphoreType.DMA((16,)),
        ],
        compiler_params=pltpu.CompilerParams(
            vmem_limit_bytes=63 << 20, collective_id=1, has_side_effects=True
        ),
    )(geometry, count, geometry, owner, soft, feat, conv_w, mask_w)
    return pl.pallas_call(
        place_kernel,
        out_shape=(
            jax.ShapeDtypeStruct((32, 32, 256), jnp.float32),
            jax.ShapeDtypeStruct((1, 1, BOX_OWN, CROP * CROP), jnp.float32),
            jax.ShapeDtypeStruct((32, 32, 256), jnp.bfloat16),
        ),
        in_specs=[S, S, V, V, V, V],
        out_specs=(V, V, H),
        scratch_shapes=[pltpu.VMEM((512, ROWS), jnp.bfloat16), pltpu.SemaphoreType.DMA((1,))],
        compiler_params=pltpu.CompilerParams(vmem_limit_bytes=63 << 20),
    )(geometry, count, geometry, grads, logits, feat)


def shards(
    tokens,
    first_gain,
    second_gain,
    joint_weight,
    merge_weight,
    expand_weight,
    shrink_weight,
    relative_bias,
    lateral_weight,
    conv_weight,
    mask_weight,
    box_geometry,
    box_counts,
    box_owner,
    soft_target,
):
    features = swin(
        tokens, first_gain, second_gain, joint_weight, merge_weight,
        expand_weight, shrink_weight, relative_bias, lateral_weight,
    )
    feature_grad, logits, features = mask_head(
        box_geometry.transpose(0, 1, 3, 2), box_counts, box_owner, soft_target, features,
        conv_weight, mask_weight,
    )
    return (features, feature_grad, logits)


def solution(mesh):
    placed = (
        P("row", "col", None),
        P(),
        P(),
        P(),
        P(),
        P(),
        P(),
        P(),
        P(),
        P(),
        P(),
        P("row", "col", None, None),
        P("row", "col"),
        P("row", "col", None),
        P("row", "col", None, None),
    )
    return jax.shard_map(
        shards,
        mesh=mesh,
        in_specs=placed,
        out_specs=(P("row", "col", None), P("row", "col", None), P("row", "col", None, None)),
        check_vma=False,
    )
```
